32 devices in a mesh: dp: 4 (over z), row: 2 (over y), col: 4 (over x, core).
Axes of the slice: x: 2, y: 2, z: 4, core: 2. Of those that a mesh axis runs over, the one named last changes fastest.
Arguments:
- layer_input: float32 [1024, 16384], P(('row', 'col'), 'dp'), may hold values from -6 to 6
- teacher: float32 [1024, 16384], P(('row', 'col'), 'dp'), may hold values from -6 to 6
- block_len: int32 [8], P('dp'), may hold values from 1 to 2048, as said below
- block_first: int32 [8], P('dp'), may hold values from 0 to 1, as said below
- norm_gain: float32 [1024], P(('row', 'col')), may hold values from 0.5 to 1.5
- norm_bias: float32 [1024], P(('row', 'col')), may hold values from -3 to 3
- ema_rate: float32 [1024, 16], P(('row', 'col')), may hold values from 0.002 to 0.1
- ema_angle: float32 [1024, 16], P(('row', 'col')), may hold values from 0 to 0.6
- ema_input: float32 [1024, 16], P(('row', 'col')), may hold values from -3 to 3
- ema_out_real: float32 [1024, 16], P(('row', 'col')), may hold values from -1 to 1
- ema_out_imag: float32 [1024, 16], P(('row', 'col')), may hold values from -1 to 1
- ema_skip: float32 [1024], P(('row', 'col')), may hold values from 0.5 to 1.5
- w_value: bfloat16 [2, 4, 128, 2048], P(None, 'col', None, 'row'), may hold values from -0.1875 to 0.1875
- w_shared: bfloat16 [2, 4, 128, 256], P(None, 'col', None, 'row'), may hold values from -0.1875 to 0.1875
- w_reset: bfloat16 [2, 4, 128, 2048], P(None, 'col', None, 'row'), may hold values from -0.1875 to 0.1875
- w_hidden: bfloat16 [2, 4, 128, 1024], P(None, 'col', None, 'row'), may hold values from -0.1875 to 0.1875
- w_update: bfloat16 [2, 4, 128, 1024], P(None, 'col', None, 'row'), may hold values from -0.1875 to 0.1875
- query_gain: float32 [256], P(('row', 'col')), may hold values from -3 to 3
- query_bias: float32 [256], P(('row', 'col')), may hold values from -3 to 3
- key_gain: float32 [256], P(('row', 'col')), may hold values from -3 to 3
- w_output: bfloat16 [2, 4, 256, 1024], P(None, 'col', None, 'row'), may hold values from -0.5 to 0.5
- final_gain: float32 [1024], P(('row', 'col')), may hold values from 0.5 to 1.5
- final_bias: float32 [1024], P(('row', 'col')), may hold values from -3 to 3
- w_gate: bfloat16 [2, 4, 128, 2560], P(None, 'col', None, 'row'), may hold values from -0.1875 to 0.1875
- w_up: bfloat16 [2, 4, 128, 2560], P(None, 'col', None, 'row'), may hold values from -0.1875 to 0.1875
- w_down: bfloat16 [2, 4, 320, 1024], P(None, 'col', None, 'row'), may hold values from -0.125 to 0.125
Outputs:
- layer_output: float32 [1024, 16384], P(('row', 'col'), 'dp')
- loss: float32 [], replicated
- input_grad: float32 [1024, 16384], P(('row', 'col'), 'dp')
- grad_norm_gain: float32 [1024], P(('row', 'col'))
- grad_norm_bias: float32 [1024], P(('row', 'col'))
- grad_ema_rate: float32 [1024, 16], P(('row', 'col'))
- grad_ema_angle: float32 [1024, 16], P(('row', 'col'))
- grad_ema_input: float32 [1024, 16], P(('row', 'col'))
- grad_ema_out_real: float32 [1024, 16], P(('row', 'col'))
- grad_ema_out_imag: float32 [1024, 16], P(('row', 'col'))
- grad_ema_skip: float32 [1024], P(('row', 'col'))
- grad_w_value: float32 [2, 4, 128, 2048], P(None, 'col', None, 'row')
- grad_w_shared: float32 [2, 4, 128, 256], P(None, 'col', None, 'row')
- grad_w_reset: float32 [2, 4, 128, 2048], P(None, 'col', None, 'row')
- grad_w_hidden: float32 [2, 4, 128, 1024], P(None, 'col', None, 'row')
- grad_w_update: float32 [2, 4, 128, 1024], P(None, 'col', None, 'row')
- grad_query_gain: float32 [256], P(('row', 'col'))
- grad_query_bias: float32 [256], P(('row', 'col'))
- grad_key_gain: float32 [256], P(('row', 'col'))
- grad_w_output: float32 [2, 4, 256, 1024], P(None, 'col', None, 'row')
- grad_final_gain: float32 [1024], P(('row', 'col'))
- grad_final_bias: float32 [1024], P(('row', 'col'))
- grad_w_gate: float32 [2, 4, 128, 2560], P(None, 'col', None, 'row')
- grad_w_up: float32 [2, 4, 128, 2560], P(None, 'col', None, 'row')
- grad_w_down: float32 [2, 4, 320, 1024], P(None, 'col', None, 'row')
The draws below stay inside these ranges and needn't reach their ends.
Inputs may be any that keep to these rules, and one draw needn't show every extreme that they name: `block_len`: the slots of each dp index form 2 aligned blocks of 2048; a sequence takes a run of whole blocks beginning at a block whose block_first is 1, and block 0 of every dp index begins one; every block except the last of a sequence of two or more blocks has all 2048 slots valid; the valid slots of a block come first. `block_first`: 1 where a block begins a sequence, 0 where it continues one.
All inputs are finite; a program needn't handle non-finite values.
Results may differ from the reference program's by a relative error of at most 0.014.
Values may be sent and summed in bfloat16 or wider, within the bound.
A program may use at most 384 MiB of HBM per device.

```python
import math
import jax
import jax.numpy as jnp
from jax import lax

D = 1024
Z = 256
V = 2048
FF = 2560
NDIM = 16
SPAN = 2048
GS = 32
SLOTS = 4096
BLOCKS = 2
TOKENS = 16384
N_DP = 4
N_ROW = 2
N_COL = 4


def sequence_layout(key):
    coin_flips = jax.random.randint(jax.random.fold_in(key, 7), (N_DP, BLOCKS), 0, 2)
    column = jnp.arange(BLOCKS, dtype=jnp.int32)[None, :]
    starts = jnp.where(column == 0, 1, coin_flips).astype(jnp.int32)
    following = jnp.concatenate([starts[:, 1:], jnp.ones((N_DP, 1), jnp.int32)], axis=1)
    partial_len = jax.random.randint(jax.random.fold_in(key, 8), (N_DP, BLOCKS), 1, SPAN + 1)
    last_of_many = (following == 1) & (starts == 0)
    lengths = jnp.where(last_of_many, partial_len, SPAN).astype(jnp.int32)
    return (starts.reshape(-1), lengths.reshape(-1))


def draw_block_first(key, part):
    return sequence_layout(key)[0]


def draw_block_len(key, part):
    return sequence_layout(key)[1]


def levels(rng, extent, shards, smallest, top_value):
    factor_of, own = 1.0, jax.random.fold_in(rng, 6)
    for axis_at, blocks in shards:
        draws = jnp.exp(jax.random.uniform(jax.random.fold_in(own, axis_at), (blocks,), jnp.float32, smallest / len(shards), top_value / len(shards)))
        factor_of = factor_of * jnp.repeat(draws, extent[axis_at] // blocks).reshape([-1 if axis == axis_at else 1 for axis in range(len(extent))])
    return factor_of


def scatter_about(rng, dims, width, most, pieces=(), kind=jnp.bfloat16):
    level = levels(rng, dims, pieces, -0.22, 0.18) if pieces else 1.0
    drawn = jax.random.normal(rng, dims, jnp.float32) * width * level
    return jnp.minimum(jnp.maximum(drawn, -most), most).astype(kind)


def setup_inputs(seed: int = 0) -> dict:
    key_of = jax.random.split(jax.random.key(seed), 27)
    return {
        "layer_input": scatter_about(key_of[0], (D, TOKENS), 1.0, 6.0, ((0, 8), (1, 4)), jnp.float32),
        "teacher": scatter_about(key_of[1], (D, TOKENS), 1.0, 6.0, ((0, 8), (1, 4)), jnp.float32),
        "block_len": draw_block_len(jax.random.fold_in(key_of[26], 71), 0),
        "block_first": draw_block_first(jax.random.fold_in(key_of[26], 71), 0),
        "norm_gain": jnp.clip(1.0 + 0.1 * jax.random.normal(key_of[4], (D,), jnp.float32), 0.5, 1.5),
        "norm_bias": scatter_about(key_of[5], (D,), 0.3, 3.0, ((0, 8),), jnp.float32),
        "ema_rate": jnp.clip(jnp.exp(math.log(0.1) - 3.912023 * jax.random.uniform(key_of[6], (D, NDIM), jnp.float32) ** levels(key_of[6], (D, NDIM), ((0, 8),), -0.2, 0.2)), 0.002, 0.1),
        "ema_angle": jnp.clip(0.6 * jax.random.uniform(key_of[7], (D, NDIM), jnp.float32) ** levels(key_of[7], (D, NDIM), ((0, 8),), -0.2, 0.2), 0.0, 0.6),
        "ema_input": scatter_about(key_of[8], (D, NDIM), 1.0, 3.0, ((0, 8),), jnp.float32),
        "ema_out_real": scatter_about(key_of[9], (D, NDIM), (2 * NDIM) ** -0.5, 1.0, ((0, 8),), jnp.float32),
        "ema_out_imag": scatter_about(key_of[10], (D, NDIM), (2 * NDIM) ** -0.5, 1.0, ((0, 8),), jnp.float32),
        "ema_skip": jnp.clip(0.5 + 1.0 * jax.random.uniform(key_of[11], (D,), jnp.float32) ** levels(key_of[11], (D,), ((0, 8),), -0.2, 0.2), 0.5, 1.5),
        "w_value": scatter_about(key_of[12], (N_ROW, N_COL, D // (N_ROW * N_COL), V), D ** -0.5, 0.1875, ((1, 4), (3, 2))),
        "w_shared": scatter_about(key_of[13], (N_ROW, N_COL, D // (N_ROW * N_COL), Z), D ** -0.5, 0.1875, ((1, 4), (3, 2))),
        "w_reset": scatter_about(key_of[14], (N_ROW, N_COL, D // (N_ROW * N_COL), V), D ** -0.5, 0.1875, ((1, 4), (3, 2))),
        "w_hidden": scatter_about(key_of[15], (N_ROW, N_COL, D // (N_ROW * N_COL), D), D ** -0.5, 0.1875, ((1, 4), (3, 2))),
        "w_update": scatter_about(key_of[16], (N_ROW, N_COL, D // (N_ROW * N_COL), D), D ** -0.5, 0.1875, ((1, 4), (3, 2))),
        "query_gain": jnp.clip(jax.random.uniform(key_of[17], (Z,), jnp.float32, -3.0, 3.0) * levels(key_of[17], (Z,), ((0, 8),), -0.4, 0.0), -3.0, 3.0),
        "query_bias": scatter_about(key_of[18], (Z,), 0.5, 3.0, ((0, 8),), jnp.float32),
        "key_gain": jnp.clip(jax.random.uniform(key_of[19], (Z,), jnp.float32, -3.0, 3.0) * levels(key_of[19], (Z,), ((0, 8),), -0.4, 0.0), -3.0, 3.0),
        "w_output": scatter_about(key_of[20], (N_ROW, N_COL, V // (N_ROW * N_COL), D), (V // 16) ** -0.5, 0.5, ((1, 4), (3, 2))),
        "final_gain": jnp.clip(1.0 + 0.1 * jax.random.normal(key_of[21], (D,), jnp.float32), 0.5, 1.5),
        "final_bias": scatter_about(key_of[22], (D,), 0.2, 3.0, ((0, 8),), jnp.float32),
        "w_gate": scatter_about(key_of[23], (N_ROW, N_COL, D // (N_ROW * N_COL), FF), D ** -0.5, 0.1875, ((1, 4), (3, 2))),
        "w_up": scatter_about(key_of[24], (N_ROW, N_COL, D // (N_ROW * N_COL), FF), D ** -0.5, 0.1875, ((1, 4), (3, 2))),
        "w_down": scatter_about(key_of[25], (N_ROW, N_COL, FF // (N_ROW * N_COL), D), FF ** -0.5, 0.125, ((1, 4), (3, 2))),
    }


@jax.custom_vjp
def low(v):
    return lax.optimization_barrier(v.astype(jnp.bfloat16)).astype(jnp.float32)

@jax.custom_vjp
def low_back(v):
    return v

def low_keep(v):
    return (low(v), None)

def low_pass(kept, grad):
    return (grad,)

def back_keep(v):
    return (v, None)

def back_low(kept, grad):
    return (low(grad),)
low.defvjp(low_keep, low_pass)
low_back.defvjp(back_keep, back_low)
EPSILON = 1e-05
NEGATIVE = -1000000000.0
PRECISE = lax.Precision.HIGHEST

def running_sums(values, first_flags, block_rows):
    height = values.shape[0]
    blocked = values.reshape(height, -1, block_rows)
    inside = jnp.cumsum(blocked, axis=2)
    totals = inside[:, :, -1]

    def carry_step(carried, scan_item):
        block_total, reset_flag = scan_item
        begin_sum = carried * (1.0 - reset_flag)
        return (begin_sum + block_total, begin_sum)
    unused, starts = lax.scan(carry_step, jnp.zeros((height,), jnp.float32), (totals.T, first_flags))
    return (inside + starts.T[:, :, None]).reshape(height, -1)

def step_norm(layer_in, norm_gain, norm_bias, first_flags):
    channels, length = layer_in.shape
    grouped = layer_in.reshape(channels // GS, GS, length)
    sum_one = running_sums(lax.optimization_barrier(jnp.sum(grouped, axis=1)), first_flags, SPAN)
    sum_two = running_sums(lax.optimization_barrier(jnp.sum(grouped * grouped, axis=1)), first_flags, SPAN)
    counted = running_sums(jnp.ones((1, length), jnp.float32), first_flags, SPAN) * GS
    mean_val = sum_one / counted
    var_val = sum_two / counted - mean_val * mean_val
    centred = (grouped - mean_val[:, None, :]) * lax.rsqrt(var_val + EPSILON)[:, None, :]
    return centred.reshape(channels, length) * norm_gain[:, None] + norm_bias[:, None]

def ema_scan(normed, ema_rate, ema_angle, ema_input, ema_out_real, ema_out_imag, resets):
    piece_len = min(128, SPAN)
    decay_rate = 1.0 - ema_rate
    turn_re = decay_rate * jnp.cos(ema_angle)
    turn_im = decay_rate * jnp.sin(ema_angle)
    in_coeff = jnp.sqrt(2.0 * ema_rate) * ema_input

    def one_step(carried, step_item):
        column, reset_flag = step_item
        state_re, state_im = carried
        keeping = 1.0 - reset_flag
        new_re = keeping * (turn_re * state_re - turn_im * state_im) + in_coeff * column[:, None]
        new_im = keeping * (turn_re * state_im + turn_im * state_re)
        return ((new_re, new_im), lax.optimization_barrier(jnp.sum(ema_out_real * new_re - ema_out_imag * new_im, axis=1)))

    def one_piece(carried, piece_item):
        return lax.scan(one_step, carried, piece_item)
    channels = normed.shape[0]
    series = normed.T.reshape(-1, piece_len, channels)
    piece_flags = resets.reshape(-1, piece_len)
    zero_state = jnp.zeros((channels, NDIM), jnp.float32)
    unused, outputs = lax.scan(jax.checkpoint(one_piece), (zero_state, zero_state), (series, piece_flags))
    return outputs.reshape(-1, channels).T

def attention(queries, keys_low, values_low):
    groups = N_ROW * N_COL
    positions = jnp.arange(SPAN)
    causal = positions[:, None] >= positions[None, :]

    def to_blocks(array_in):
        return array_in.reshape(array_in.shape[0], -1, SPAN).transpose(1, 0, 2)

    def per_block(block_item):
        query_blk, key_blk, value_blk = block_item
        raw_scores = jnp.dot(query_blk.T, key_blk, precision=PRECISE, preferred_element_type=jnp.float32) * Z ** (-0.5)
        scores = jnp.where(causal, raw_scores, NEGATIVE)

        def per_group(value_grp):
            rounded = low_back(scores)
            top_score = lax.optimization_barrier(jnp.max(rounded, axis=1, keepdims=True))
            exponent = jnp.exp(rounded - top_score)
            prob_rows = exponent / lax.optimization_barrier(jnp.sum(exponent, axis=1, keepdims=True))
            return jnp.dot(value_grp, low(prob_rows).T, precision=PRECISE, preferred_element_type=jnp.float32)
        return lax.map(jax.checkpoint(per_group), value_blk.reshape(groups, -1, SPAN)).reshape(-1, SPAN)
    mapped = lax.map(jax.checkpoint(per_block), (to_blocks(queries), to_blocks(keys_low), to_blocks(values_low)))
    return mapped.transpose(1, 0, 2).reshape(values_low.shape[0], -1)

def project(weight, source):
    matrix = weight.reshape(-1, weight.shape[-1])
    return jnp.dot(matrix.T, source, precision=PRECISE, preferred_element_type=jnp.float32)

def group_forward(slab_in, target, valid_row, first_row, valid_total, params):
    norm_gain, norm_bias, ema_rate, ema_angle, ema_input, ema_out_real, ema_out_imag, ema_skip, w_value, w_shared, w_reset, w_hidden, w_update, query_gain, query_bias, key_gain, w_output, final_gain, final_bias, w_gate, w_up, w_down = params
    resets = (jnp.arange(SLOTS) % SPAN == 0) * jnp.repeat(first_row, SPAN)
    normed = step_norm(slab_in, norm_gain, norm_bias, first_row)
    smoothed = ema_scan(normed, ema_rate, ema_angle, ema_input, ema_out_real, ema_out_imag, resets)
    mixed_act = jax.nn.silu(smoothed + ema_skip[:, None] * normed)
    normed_low = low(normed)
    mixed_low = low(mixed_act)
    value_pre = low_back(project(w_value, normed_low))
    shared = low_back(project(w_shared, mixed_low))
    reset_pre = low_back(project(w_reset, mixed_low))
    update_pre = low_back(project(w_update, mixed_low))
    hidden_pre = project(w_hidden, mixed_low)
    values_low = low(jax.nn.silu(value_pre))
    queries = low(shared * query_gain[:, None] + query_bias[:, None])
    keys_low = low(shared * key_gain[:, None])
    attended = low_back(attention(queries, keys_low, values_low))
    att_in = low(attended * jax.nn.silu(reset_pre))
    summed = low_back(hidden_pre + project(w_output, att_in))
    gate_act = jax.nn.sigmoid(update_pre)
    first_out = slab_in + gate_act * (jax.nn.silu(summed) - slab_in)
    mean_val = lax.optimization_barrier(jnp.mean(first_out, axis=0))
    var_val = lax.optimization_barrier(jnp.mean(first_out * first_out, axis=0)) - mean_val * mean_val
    unit_norm = (first_out - mean_val) * lax.rsqrt(var_val + EPSILON)
    final_norm = low(unit_norm * final_gain[:, None] + final_bias[:, None])
    gate_pre = low_back(project(w_gate, final_norm))
    up_pre = low_back(project(w_up, final_norm))
    inner_act = low(jax.nn.silu(gate_pre) * up_pre)
    layer_out = first_out + low_back(project(w_down, inner_act))
    out_error = (layer_out - target) * valid_row[None, :]
    return (layer_out, jnp.sum(out_error * out_error) / (2.0 * valid_total * D))

def reference(layer_input, teacher, block_len, block_first, norm_gain, norm_bias, ema_rate, ema_angle, ema_input, ema_out_real, ema_out_imag, ema_skip, w_value, w_shared, w_reset, w_hidden, w_update, query_gain, query_bias, key_gain, w_output, final_gain, final_bias, w_gate, w_up, w_down):
    params = (norm_gain, norm_bias, ema_rate, ema_angle, ema_input, ema_out_real, ema_out_imag, ema_skip, w_value.astype(jnp.float32), w_shared.astype(jnp.float32), w_reset.astype(jnp.float32), w_hidden.astype(jnp.float32), w_update.astype(jnp.float32), query_gain, query_bias, key_gain, w_output.astype(jnp.float32), final_gain, final_bias, w_gate.astype(jnp.float32), w_up.astype(jnp.float32), w_down.astype(jnp.float32))
    slot_index = jnp.arange(TOKENS)
    valid_mask = (slot_index % SPAN < jnp.repeat(block_len, SPAN)).astype(jnp.float32)
    valid_total = jnp.sum(valid_mask)
    slab_list = layer_input.reshape(D, N_DP, SLOTS).transpose(1, 0, 2)
    targets = teacher.reshape(D, N_DP, SLOTS).transpose(1, 0, 2)
    valid_rows = valid_mask.reshape(N_DP, SLOTS)
    first_rows = block_first.reshape(N_DP, BLOCKS).astype(jnp.float32)

    def per_index(carried, group_item):
        grad_sums, loss_sum = carried
        slab_in, target, valid_row, first_row = group_item

        def objective(slab_arg, param_arg):
            return group_forward(slab_arg, target, valid_row, first_row, valid_total, param_arg)
        (layer_out, loss_part), pullback = jax.vjp(objective, slab_in, params)
        slab_grad, param_grads = pullback((jnp.zeros_like(layer_out), jnp.ones_like(loss_part) * (TOKENS * D)))
        grad_sums = jax.tree.map(lambda running, addend: running + addend, grad_sums, param_grads)
        return ((grad_sums, loss_sum + loss_part), (layer_out, slab_grad))
    start_sums = jax.tree.map(jnp.zeros_like, params)
    (grad_sums, loss_total), (outputs, input_grads) = lax.scan(per_index, (start_sums, jnp.zeros((), jnp.float32)), (slab_list, targets, valid_rows, first_rows))
    layer_output = outputs.transpose(1, 0, 2).reshape(D, TOKENS)
    input_grad = input_grads.transpose(1, 0, 2).reshape(D, TOKENS)
    return (layer_output, loss_total, input_grad, grad_sums[0], grad_sums[1], grad_sums[2], grad_sums[3], grad_sums[4], grad_sums[5], grad_sums[6], grad_sums[7], grad_sums[8], grad_sums[9], grad_sums[10], grad_sums[11], grad_sums[12], grad_sums[13], grad_sums[14], grad_sums[15], grad_sums[16], grad_sums[17], grad_sums[18], grad_sums[19], grad_sums[20], grad_sums[21])
```

```python
from functools import partial

import jax
import jax.numpy as jnp
from jax import lax
from jax.sharding import PartitionSpec as P

D = 1024
Z = 256
SPAN = 2048
GS = 32


EPSILON = 1e-05
NEGATIVE = -1000000000.0
PRECISE = lax.Precision.HIGHEST


def running_sums(values, first_flags, block_rows):
    height = values.shape[0]
    blocked = values.reshape(height, -1, block_rows)
    inside = jnp.cumsum(blocked, axis=2)
    totals = inside[:, :, -1]

    def carry_step(carried, scan_item):
        block_total, reset_flag = scan_item
        begin_sum = carried * (1.0 - reset_flag)
        return (begin_sum + block_total, begin_sum)

    unused, starts = lax.scan(
        carry_step, jnp.zeros((height,), jnp.float32), (totals.T, first_flags)
    )
    return (inside + starts.T[:, :, None]).reshape(height, -1)


def step_norm(layer_in, norm_gain, norm_bias, first_flags):
    channels, length = layer_in.shape
    grouped = layer_in.reshape(channels // GS, GS, length)
    sum_one = running_sums(jnp.sum(grouped, axis=1), first_flags, SPAN)
    sum_two = running_sums(jnp.sum(grouped * grouped, axis=1), first_flags, SPAN)
    counted = running_sums(jnp.ones((1, length), jnp.float32), first_flags, SPAN) * GS
    mean_val = sum_one / counted
    var_val = sum_two / counted - mean_val * mean_val
    centred = (grouped - mean_val[:, None, :]) * lax.rsqrt(var_val + EPSILON)[:, None, :]
    return centred.reshape(channels, length) * norm_gain[:, None] + norm_bias[:, None]


def silu_slope(pre_act):
    logistic = jax.nn.sigmoid(pre_act)
    return logistic * (1.0 + pre_act * (1.0 - logistic))


def contract_first(left_in, right_in):
    return lax.dot_general(
        left_in, right_in, (((0,), (0,)), ((), ())), preferred_element_type=jnp.float32
    )


def contract_last(left_in, right_in):
    return lax.dot_general(
        left_in, right_in, (((1,), (1,)), ((), ())), preferred_element_type=jnp.float32
    )


def ema_blocks(normed, ema_rate, ema_angle, ema_input, ema_out_real, ema_out_imag, piece_resets):
    piece_len = min(128, SPAN)
    channels, slot_count = normed.shape
    decay_rate = 1.0 - ema_rate
    in_coeff = jnp.sqrt(2.0 * ema_rate) * ema_input
    powers = jnp.arange(piece_len + 1, dtype=jnp.float32)[:, None, None]
    magnitude = jnp.exp(powers * jnp.log(decay_rate)[None])
    phases = powers * ema_angle[None]
    power_re = magnitude * jnp.cos(phases)
    power_im = magnitude * jnp.sin(phases)
    mixed_re = ema_out_real[None] * power_re - ema_out_imag[None] * power_im
    mixed_im = ema_out_real[None] * power_im + ema_out_imag[None] * power_re
    kernel = jnp.sum(in_coeff[None] * mixed_re[:piece_len], axis=2)
    offsets = jnp.arange(piece_len)[:, None] - jnp.arange(piece_len)[None, :]
    toeplitz = jnp.where(offsets[None] >= 0, kernel.T[:, jnp.maximum(offsets, 0)], 0.0)
    pieces = normed.reshape(channels, -1, piece_len)
    inside = jnp.einsum("cts,cbs->cbt", toeplitz, pieces, precision=PRECISE)
    back_re = power_re[:piece_len][::-1] * in_coeff[None]
    back_im = power_im[:piece_len][::-1] * in_coeff[None]
    ends_re = jnp.einsum("scj,cbs->cbj", back_re, pieces, precision=PRECISE)
    ends_im = jnp.einsum("scj,cbs->cbj", back_im, pieces, precision=PRECISE)
    keeping = (1.0 - piece_resets)[None, :, None]
    step_re = keeping * power_re[piece_len][:, None, :]
    step_im = keeping * power_im[piece_len][:, None, :]

    def combine(earlier, following):
        head_mre, head_mim, head_are, head_aim = earlier
        tail_mre, tail_mim, tail_are, tail_aim = following
        return (
            tail_mre * head_mre - tail_mim * head_mim,
            tail_mre * head_mim + tail_mim * head_mre,
            tail_mre * head_are - tail_mim * head_aim + tail_are,
            tail_mre * head_aim + tail_mim * head_are + tail_aim,
        )

    scanned = lax.associative_scan(combine, (step_re, step_im, ends_re, ends_im), axis=1)
    state_re = (
        jnp.concatenate([jnp.zeros_like(ends_re[:, :1]), scanned[2][:, :-1]], axis=1) * keeping
    )
    state_im = (
        jnp.concatenate([jnp.zeros_like(ends_im[:, :1]), scanned[3][:, :-1]], axis=1) * keeping
    )
    across = jnp.einsum("tcj,cbj->cbt", mixed_re[1:], state_re, precision=PRECISE) - jnp.einsum(
        "tcj,cbj->cbt", mixed_im[1:], state_im, precision=PRECISE
    )
    return (inside + across).reshape(channels, slot_count)


def front_piece(
    first_flags,
    piece_resets,
    layer_in,
    norm_gain,
    norm_bias,
    ema_rate,
    ema_angle,
    ema_input,
    ema_out_real,
    ema_out_imag,
    ema_skip,
):
    normed = step_norm(layer_in, norm_gain, norm_bias, first_flags)
    smoothed = ema_blocks(
        normed, ema_rate, ema_angle, ema_input, ema_out_real, ema_out_imag, piece_resets
    )
    return (normed, jax.nn.silu(smoothed + ema_skip[:, None] * normed))


def silu(pre_act):
    return pre_act * jax.nn.sigmoid(pre_act)


def swap_blocks(array_in, outer, inner):
    shaped = array_in.reshape(outer, inner, -1, array_in.shape[-1])
    return shaped.transpose(1, 0, 2, 3).reshape(array_in.shape)


def project(weights, source):
    return jnp.concatenate(
        [contract_first(weights[part], source) for part in range(weights.shape[0])], axis=0
    )


def project_back(weights, grads):
    parts = weights.shape[0]
    pieces = grads.reshape(parts, -1, grads.shape[-1])
    total = None
    for part in range(parts):
        product = jnp.dot(weights[part], pieces[part], preferred_element_type=jnp.float32)
        total = product if total is None else total + product
    return total


def weight_products(source, grads, parts):
    pieces = grads.reshape(parts, -1, grads.shape[-1])
    return [contract_last(source, pieces[part]).astype(jnp.bfloat16) for part in range(parts)]


def shards(
    layer_input,
    teacher,
    block_len,
    block_first,
    norm_gain,
    norm_bias,
    ema_rate,
    ema_angle,
    ema_input,
    ema_out_real,
    ema_out_imag,
    ema_skip,
    w_value,
    w_shared,
    w_reset,
    w_hidden,
    w_update,
    query_gain,
    query_bias,
    key_gain,
    w_output,
    final_gain,
    final_bias,
    w_gate,
    w_up,
    w_down,
):
    bf16 = jnp.bfloat16
    grid = ("row", "col")
    rows, cols, dps = lax.axis_size("row"), lax.axis_size("col"), lax.axis_size("dp")
    devices = rows * cols
    slot_count = layer_input.shape[1]
    blocks_here = slot_count // SPAN
    group = devices // blocks_here
    tokens = slot_count // devices
    half = tokens // 2
    place = lax.axis_index("row") * cols + lax.axis_index("col")
    my_block = place // group
    member = place % group
    piece_len = min(128, SPAN)
    per_block = SPAN // piece_len
    first_flags = block_first.astype(jnp.float32)
    piece_resets = jnp.repeat(first_flags, per_block) * (
        jnp.arange(slot_count // piece_len) % per_block == 0
    )

    def deal(array_in):
        feats = array_in.shape[0]
        shaped = array_in.reshape(feats, blocks_here, 2, group, half)
        paired = jnp.stack([shaped[:, :, 0], shaped[:, :, 1, ::-1]], axis=3)
        return paired.reshape(feats, slot_count)

    def undeal(array_in):
        feats = array_in.shape[0]
        shaped = array_in.reshape(feats, blocks_here, group, 2, half)
        paired = jnp.stack([shaped[:, :, :, 0], shaped[:, :, ::-1, 1]], axis=2)
        return paired.reshape(feats, slot_count)

    def to_slots(array_in):
        return lax.all_to_all(deal(array_in), grid, 1, 0, tiled=True)

    def to_features(array_in):
        return undeal(lax.all_to_all(array_in, grid, 0, 1, tiled=True))

    def gather_weights(local):
        gathered = lax.all_gather(local, grid, axis=0)
        return gathered.reshape(rows, -1, local.shape[-1])

    def local_matrix(weight_list):
        flat = [weight.reshape(-1, weight.shape[-1]) for weight in weight_list]
        return flat[0] if len(flat) == 1 else jnp.concatenate(flat, axis=1)

    front_weights = gather_weights(local_matrix([w_value, w_shared, w_reset, w_hidden, w_update]))
    output_weights = gather_weights(local_matrix([w_output]))
    inner_weights = gather_weights(local_matrix([w_gate, w_up]))
    down_weights = gather_weights(local_matrix([w_down]))
    vectors = lax.all_gather(
        jnp.concatenate([final_gain, final_bias, query_gain, query_bias, key_gain]), grid, axis=0
    )
    feat_share, z_share = final_gain.shape[0], query_gain.shape[0]

    def whole_vector(start, share):
        return vectors[:, start : start + share].reshape(-1)

    gain_all = whole_vector(0, feat_share)
    bias_all = whole_vector(feat_share, feat_share)
    query_gain_all = whole_vector(2 * feat_share, z_share)
    query_bias_all = whole_vector(2 * feat_share + z_share, z_share)
    key_gain_all = whole_vector(2 * feat_share + 2 * z_share, z_share)

    valid_total = lax.psum(jnp.sum(block_len), "dp").astype(jnp.float32)
    positions = jnp.concatenate(
        [member * half + jnp.arange(half), (2 * group - 1 - member) * half + jnp.arange(half)]
    )
    valid_mask = (positions < block_len[my_block]).astype(jnp.float32)
    members = jnp.arange(group)[:, None]
    inside = jnp.arange(half)[None, :]
    key_positions = jnp.stack(
        [members * half + inside, (2 * group - 1 - members) * half + inside], axis=1
    ).reshape(-1)

    front_out, front_pull = jax.vjp(
        partial(front_piece, first_flags, piece_resets),
        layer_input,
        norm_gain,
        norm_bias,
        ema_rate,
        ema_angle,
        ema_input,
        ema_out_real,
        ema_out_imag,
        ema_skip,
    )
    normed, mixed_act = front_out
    sources = lax.all_to_all(
        jnp.stack([deal(normed.astype(bf16)), deal(mixed_act.astype(bf16))]), grid, 2, 1, tiled=True
    )
    normed_low = swap_blocks(sources[0], rows, cols)
    mixed_low = swap_blocks(sources[1], rows, cols)
    n_value, n_shared, n_reset, n_hidden = (
        weight.shape[-1] for weight in (w_value, w_shared, w_reset, w_hidden)
    )
    value_pre = project(front_weights[:, :, :n_value], normed_low)
    mixed_out = [
        contract_first(front_weights[part, :, n_value:], mixed_low) for part in range(rows)
    ]

    def mixed_slice(start, count):
        return jnp.concatenate([piece[start : start + count] for piece in mixed_out], axis=0)

    shared = mixed_slice(0, n_shared)
    reset_pre = mixed_slice(n_shared, n_reset)
    hidden_pre = mixed_slice(n_shared + n_reset, n_hidden)
    update_pre = mixed_slice(n_shared + n_reset + n_hidden, n_hidden)
    values_low = silu(value_pre).astype(bf16)
    queries = (shared * query_gain_all[:, None] + query_bias_all[:, None]).astype(bf16)
    keys_low = (shared * key_gain_all[:, None]).astype(bf16)
    key_values = jnp.concatenate([values_low, keys_low], axis=0)
    if rows == blocks_here:
        gathered_kv = lax.all_gather(key_values, "col", axis=0)
    else:
        gathered_kv = lax.dynamic_slice_in_dim(
            lax.all_gather(key_values, grid, axis=0), my_block * group, group, 0
        )
    gathered_kv = gathered_kv.transpose(1, 0, 2).reshape(key_values.shape[0], -1)
    width = values_low.shape[0]
    value_all, key_all = gathered_kv[:width], gathered_kv[width:]
    input_slots = to_slots(layer_input)
    teacher_slots = to_slots(teacher)

    score_scale = Z ** (-0.5)
    causal = positions[:, None] >= key_positions[None, :]
    scores = jnp.where(causal, contract_first(queries, key_all) * score_scale, NEGATIVE)
    top_score = jnp.max(scores, axis=1, keepdims=True)
    exponent = jnp.exp(scores - top_score)
    probs = exponent / jnp.sum(exponent, axis=1, keepdims=True)
    probs_low = probs.astype(bf16)
    attended = contract_last(value_all, probs_low)
    reset_act = silu(reset_pre)
    att_in = swap_blocks((attended * reset_act).astype(bf16), rows, cols)
    summed = hidden_pre + project(output_weights, att_in)
    hidden_act = silu(summed)
    gate_act = jax.nn.sigmoid(update_pre)
    first_out = input_slots + gate_act * (hidden_act - input_slots)
    mean_val = jnp.mean(first_out, axis=0)
    inv_std = lax.rsqrt(jnp.mean(first_out * first_out, axis=0) - mean_val * mean_val + EPSILON)
    unit_norm = (first_out - mean_val) * inv_std
    final_norm = swap_blocks(
        (unit_norm * gain_all[:, None] + bias_all[:, None]).astype(bf16), rows, cols
    )
    n_inner = w_gate.shape[-1]
    inner_out = [contract_first(inner_weights[part], final_norm) for part in range(rows)]
    gate_pre = jnp.concatenate([piece[:n_inner] for piece in inner_out], axis=0)
    up_pre = jnp.concatenate([piece[n_inner:] for piece in inner_out], axis=0)
    inner_act = swap_blocks((silu(gate_pre) * up_pre).astype(bf16), rows, cols)
    output_slots = first_out + project(down_weights, inner_act)
    out_error = (output_slots - teacher_slots) * valid_mask
    loss_part = jnp.sum(out_error * out_error)
    out_grad = out_error * (slot_count * dps / valid_total)
    layer_output = to_features(output_slots)

    out_low = out_grad.astype(bf16)
    inner_grad = swap_blocks(project_back(down_weights, out_low), cols, rows)
    gate_grad = (inner_grad * up_pre * silu_slope(gate_pre)).astype(bf16)
    up_grad = (inner_grad * silu(gate_pre)).astype(bf16)
    inner_grads = jnp.concatenate(
        [gate_grad.reshape(rows, -1, tokens), up_grad.reshape(rows, -1, tokens)], axis=1
    )
    norm_grad = swap_blocks(
        project_back(inner_weights, inner_grads.reshape(-1, tokens)), cols, rows
    )

    def scatter_weight(product_list, rank):
        stacked = jnp.stack(product_list)
        shaped = stacked.reshape(devices, rows * rank, stacked.shape[-1])
        return lax.psum_scatter(shaped, grid, scatter_dimension=0, tiled=True)[0]

    down_sum = scatter_weight(weight_products(inner_act, out_low, rows), w_down.shape[2])
    inner_sum = scatter_weight(weight_products(final_norm, inner_grads, rows), w_gate.shape[2])
    down_sum, inner_sum = lax.psum((down_sum, inner_sum), "dp")

    final_gain_part = jnp.sum(norm_grad * unit_norm, axis=1)
    final_bias_part = jnp.sum(norm_grad, axis=1)
    unit_grad = norm_grad * gain_all[:, None]
    first_grad = out_grad + inv_std * (
        unit_grad
        - jnp.mean(unit_grad, axis=0)
        - unit_norm * jnp.mean(unit_grad * unit_norm, axis=0)
    )
    residual_grad = to_features(first_grad * (1.0 - gate_act))
    update_grad = (first_grad * (hidden_act - input_slots) * gate_act * (1.0 - gate_act)).astype(
        bf16
    )
    summed_grad = (first_grad * gate_act * silu_slope(summed)).astype(bf16)
    att_grad = swap_blocks(project_back(output_weights, summed_grad), cols, rows)
    attended_grad = (att_grad * reset_act).astype(bf16)
    reset_grad = (att_grad * attended * silu_slope(reset_pre)).astype(bf16)
    prob_grad = contract_first(attended_grad, value_all)
    row_dot = jnp.sum(probs * prob_grad, axis=1, keepdims=True)
    score_grad = (probs * (prob_grad - row_dot)).astype(bf16)
    query_grad = contract_last(key_all, score_grad) * score_scale
    key_grad = jnp.dot(queries, score_grad, preferred_element_type=jnp.float32) * score_scale
    value_grad = jnp.dot(attended_grad, probs_low, preferred_element_type=jnp.float32)
    kv_parts = jnp.concatenate([value_grad, key_grad], axis=0).astype(bf16)
    kv_parts = kv_parts.reshape(-1, group, tokens).transpose(1, 0, 2)
    if rows == blocks_here:
        kv_grads = lax.psum_scatter(kv_parts, "col", scatter_dimension=0, tiled=True)[0]
    else:
        spread = lax.dynamic_update_slice_in_dim(
            jnp.zeros((devices,) + kv_parts.shape[1:], bf16), kv_parts, my_block * group, 0
        )
        kv_grads = lax.psum_scatter(spread, grid, scatter_dimension=0, tiled=True)[0]
    value_grad, key_grad = kv_grads[:width].astype(jnp.float32), kv_grads[width:].astype(jnp.float32)
    value_pre_grad = (value_grad * silu_slope(value_pre)).astype(bf16)
    shared_grad = (
        query_grad * query_gain_all[:, None] + key_grad * key_gain_all[:, None]
    ).astype(bf16)
    query_gain_part = jnp.sum(query_grad * shared, axis=1)
    query_bias_part = jnp.sum(query_grad, axis=1)
    key_gain_part = jnp.sum(key_grad * shared, axis=1)
    mixed_grads = jnp.concatenate(
        [
            piece.reshape(rows, -1, tokens)
            for piece in (shared_grad, reset_grad, summed_grad, update_grad)
        ],
        axis=1,
    )
    normed_back = swap_blocks(
        project_back(front_weights[:, :, :n_value], value_pre_grad), cols, rows
    )
    mixed_back = swap_blocks(
        project_back(front_weights[:, :, n_value:], mixed_grads.reshape(-1, tokens)), cols, rows
    )
    backs = lax.all_to_all(
        jnp.stack([normed_back, mixed_back]).astype(bf16), grid, 1, 2, tiled=True
    ).astype(jnp.float32)
    input_pulls = front_pull((undeal(backs[0]), undeal(backs[1])))
    input_grad = residual_grad + input_pulls[0]

    output_sum = scatter_weight(weight_products(att_in, summed_grad, rows), w_output.shape[2])
    front_products = [
        jnp.concatenate(pair, axis=1)
        for pair in zip(
            weight_products(normed_low, value_pre_grad, rows),
            weight_products(mixed_low, mixed_grads, rows),
        )
    ]
    front_sum = scatter_weight(front_products, w_value.shape[2])
    output_sum, front_sum, down_sum = lax.optimization_barrier((output_sum, front_sum, down_sum))
    output_sum, front_sum = lax.psum((output_sum, front_sum), "dp")

    small = lax.psum(
        jnp.concatenate(
            [
                final_gain_part,
                final_bias_part,
                query_gain_part,
                query_bias_part,
                key_gain_part,
                loss_part[None],
            ]
        ),
        ("dp", "row", "col"),
    )
    loss_value = small[-1] / (2.0 * valid_total * D)

    def my_share(start, share):
        return lax.dynamic_slice_in_dim(small, start + place * share, share, 0)

    z_size = share_total = z_share * devices
    feat_size = feat_share * devices
    param_sums = lax.psum(input_pulls[1:], "dp")

    def split_columns(array_in, weight_list):
        results = []
        offset = 0
        for weight in weight_list:
            count = weight.shape[-1]
            piece = array_in[:, offset : offset + count].astype(jnp.float32)
            results.append(piece.reshape(weight.shape))
            offset += count
        return results

    value_g, shared_g, reset_g, hidden_g, update_g = split_columns(
        front_sum, [w_value, w_shared, w_reset, w_hidden, w_update]
    )
    (output_g,) = split_columns(output_sum, [w_output])
    gate_g, up_g = split_columns(inner_sum, [w_gate, w_up])
    (down_g,) = split_columns(down_sum, [w_down])
    return (
        layer_output,
        loss_value,
        input_grad,
        *param_sums,
        value_g,
        shared_g,
        reset_g,
        hidden_g,
        update_g,
        my_share(2 * feat_size, z_share),
        my_share(2 * feat_size + z_size, z_share),
        my_share(2 * feat_size + 2 * z_size, z_share),
        output_g,
        my_share(0, feat_share),
        my_share(feat_size, feat_share),
        gate_g,
        up_g,
        down_g,
    )


def solution(mesh):
    in_specs = (
        P(("row", "col"), "dp"),
        P(("row", "col"), "dp"),
        P("dp"),
        P("dp"),
        P(("row", "col")),
        P(("row", "col")),
        P(("row", "col"), None),
        P(("row", "col"), None),
        P(("row", "col"), None),
        P(("row", "col"), None),
        P(("row", "col"), None),
        P(("row", "col")),
        P(None, "col", None, "row"),
        P(None, "col", None, "row"),
        P(None, "col", None, "row"),
        P(None, "col", None, "row"),
        P(None, "col", None, "row"),
        P(("row", "col")),
        P(("row", "col")),
        P(("row", "col")),
        P(None, "col", None, "row"),
        P(("row", "col")),
        P(("row", "col")),
        P(None, "col", None, "row"),
        P(None, "col", None, "row"),
        P(None, "col", None, "row"),
    )
    out_specs = (
        P(("row", "col"), "dp"),
        P(),
        P(("row", "col"), "dp"),
        P(("row", "col")),
        P(("row", "col")),
        P(("row", "col"), None),
        P(("row", "col"), None),
        P(("row", "col"), None),
        P(("row", "col"), None),
        P(("row", "col"), None),
        P(("row", "col")),
        P(None, "col", None, "row"),
        P(None, "col", None, "row"),
        P(None, "col", None, "row"),
        P(None, "col", None, "row"),
        P(None, "col", None, "row"),
        P(("row", "col")),
        P(("row", "col")),
        P(("row", "col")),
        P(None, "col", None, "row"),
        P(("row", "col")),
        P(("row", "col")),
        P(None, "col", None, "row"),
        P(None, "col", None, "row"),
        P(None, "col", None, "row"),
    )
    return jax.shard_map(shards, mesh=mesh, in_specs=in_specs, out_specs=out_specs, check_vma=False)
```

```python
from functools import partial

import jax
import jax.numpy as jnp
from jax import lax
from jax.experimental import pallas as pl
from jax.experimental.pallas import tpu as pltpu
from jax.sharding import PartitionSpec as P

D = 1024
Z = 256
SPAN = 2048
GS = 32
UNIT = 128
STATES = 16
COUNT_ROWS = 256
BATCH = 16
BATCH_BACK = 16

EPSILON = 1e-05
NEGATIVE = -1000000000.0


NT = (((1,), (1,)), ((), ()))
NN = (((1,), (0,)), ((), ()))
TN = (((0,), (0,)), ((), ()))


def halves(array_in):
    high = array_in.astype(jnp.bfloat16)
    return high, (array_in - high.astype(jnp.float32)).astype(jnp.bfloat16)


def dot_split(left, right, dims):
    left_high, left_low = left
    right_high, right_low = right
    product = partial(lax.dot_general, dimension_numbers=dims, preferred_element_type=jnp.float32)
    return (
        product(left_high, right_high)
        + product(left_low, right_high)
        + product(left_high, right_low)
    )


def dot_exact(left, right):
    return lax.dot_general(
        left, right, NN, precision=lax.Precision.HIGHEST, preferred_element_type=jnp.float32
    )


def toeplitz(kernel_row):
    rows = lax.broadcasted_iota(jnp.int32, (UNIT, UNIT), 0)
    lanes = lax.broadcasted_iota(jnp.int32, (UNIT, UNIT), 1)
    spread = pltpu.roll(
        jnp.broadcast_to(kernel_row, (UNIT, UNIT)), 0, 1, stride=1, stride_axis=0
    )
    return jnp.where(lanes >= rows, spread, 0.0)


def lag_sums(products):
    rows = lax.broadcasted_iota(jnp.int32, (UNIT, UNIT), 0)
    lanes = lax.broadcasted_iota(jnp.int32, (UNIT, UNIT), 1)
    kept = jnp.where(rows + lanes >= UNIT - 1, products, 0.0)
    aligned = pltpu.roll(kept, 0, 1, stride=1, stride_axis=0)
    return pltpu.roll(jnp.sum(aligned, axis=0, keepdims=True), 1, 1)


def reversed_lanes(parts):
    rows = lax.broadcasted_iota(jnp.int32, (UNIT, UNIT), 0)
    lanes = lax.broadcasted_iota(jnp.int32, (UNIT, UNIT), 1)
    mirror = (rows + lanes == UNIT - 1).astype(jnp.bfloat16)
    return tuple(
        lax.dot_general(part, mirror, NN, preferred_element_type=jnp.float32).astype(jnp.bfloat16)
        for part in parts
    )


def power_tables(turn_re, turn_im):
    lanes = lax.broadcasted_iota(jnp.int32, (STATES, UNIT), 1)
    now_re = jnp.broadcast_to(turn_re, (STATES, UNIT))
    now_im = jnp.broadcast_to(turn_im, (STATES, UNIT))
    up_re = jnp.ones((STATES, UNIT), jnp.float32)
    up_im = jnp.zeros((STATES, UNIT), jnp.float32)
    down_re, down_im = up_re, up_im
    for bit in range(UNIT.bit_length() - 1):
        is_set = ((lanes >> bit) & 1) == 1
        next_re = up_re * now_re - up_im * now_im
        next_im = up_re * now_im + up_im * now_re
        fall_re = down_re * now_re - down_im * now_im
        fall_im = down_re * now_im + down_im * now_re
        up_re, up_im = jnp.where(is_set, next_re, up_re), jnp.where(is_set, next_im, up_im)
        down_re = jnp.where(is_set, down_re, fall_re)
        down_im = jnp.where(is_set, down_im, fall_im)
        now_re, now_im = now_re * now_re - now_im * now_im, 2.0 * now_re * now_im
    return up_re, up_im, down_re, down_im, now_re, now_im


def state_scan(ends_re, ends_im, leap_re, leap_im, allowed, units, sign):
    lanes = lax.broadcasted_iota(jnp.int32, ends_re.shape, 1)
    distance = 1
    while distance < units:
        shift = distance if sign > 0 else units - distance
        past_re = pltpu.roll(ends_re, shift, 1)
        past_im = pltpu.roll(ends_im, shift, 1)
        keep = allowed(lanes, distance)
        past_re = jnp.where(keep, past_re, 0.0)
        past_im = jnp.where(keep, past_im, 0.0)
        ends_re, ends_im = (
            ends_re + leap_re * past_re - leap_im * past_im,
            ends_im + leap_re * past_im + leap_im * past_re,
        )
        leap_re, leap_im = leap_re * leap_re - leap_im * leap_im, 2.0 * leap_re * leap_im
        distance *= 2
    shift = 1 if sign > 0 else units - 1
    keep = allowed(lanes, 1)
    return (
        jnp.where(keep, pltpu.roll(ends_re, shift, 1), 0.0),
        jnp.where(keep, pltpu.roll(ends_im, shift, 1), 0.0),
    )


def front_forward_kernel(
    places,
    units,
    start_row,
    start_col,
    x_ref,
    teacher_ref,
    state_ref,
    channel_ref,
    send_ref,
    plain_ref,
    pre_ref,
    stat_ref,
    table_ref,
    row_ref,
    hold_ref,
    normed_ref,
    sums_ref,
    ends_ref,
):
    f32 = jnp.float32
    rows = lax.broadcasted_iota(jnp.int32, (UNIT, UNIT), 0)
    lanes = lax.broadcasted_iota(jnp.int32, (UNIT, UNIT), 1)
    upper = (rows <= lanes).astype(f32)
    for unit in range(units):
        tile = x_ref[:, unit * UNIT : (unit + 1) * UNIT]
        sums_ref[unit : unit + 1, :] = jnp.sum(tile, axis=0, keepdims=True)
        sums_ref[units + unit : units + unit + 1, :] = jnp.sum(tile * tile, axis=0, keepdims=True)
    inside = dot_exact(sums_ref[...], upper)
    starts = start_col[...]
    later = lax.broadcasted_iota(jnp.int32, (units, units), 0)
    sooner = lax.broadcasted_iota(jnp.int32, (units, units), 1)
    before = ((sooner < later) & (sooner >= starts)).astype(f32)
    totals = jnp.broadcast_to(inside[:, UNIT - 1 : UNIT], (2 * units, UNIT))
    sum_one = inside[:units] + dot_exact(before, totals[:units])
    sum_two = inside[units:] + dot_exact(before, totals[units:])
    unit_at = lax.broadcasted_iota(jnp.int32, (units, UNIT), 0)
    lane_at = lax.broadcasted_iota(jnp.int32, (units, UNIT), 1)
    counted = (GS * ((unit_at - starts) * UNIT + lane_at + 1)).astype(f32)
    mean_val = sum_one / counted
    inv_std = lax.rsqrt(sum_two / counted - mean_val * mean_val + EPSILON)
    stat_ref[0, :units, :] = mean_val
    stat_ref[0, units:, :] = inv_std
    gain, bias, skip = channel_ref[:, 0:1], channel_ref[:, 1:2], channel_ref[:, 2:3]
    for unit in range(units):
        tile = x_ref[:, unit * UNIT : (unit + 1) * UNIT]
        mean_row = stat_ref[0, unit : unit + 1, :]
        std_row = stat_ref[0, units + unit : units + unit + 1, :]
        normed_ref[unit * GS : (unit + 1) * GS, :] = (tile - mean_row) * std_row * gain + bias

    def first_pass(step, unused):
        first = step * BATCH
        many = range(BATCH)
        base = pl.multiple_of(first * STATES, BATCH * STATES)
        params = [state_ref[pl.ds(base + one * STATES, STATES), :] for one in many]
        series = [halves(normed_ref[pl.ds(first + one, units, stride=GS), :]) for one in many]
        tables = [power_tables(params[one][:, 0:1], params[one][:, 1:2]) for one in many]
        ends, mixers, matrices, kernel_rows = [], [], [], []
        for one in many:
            turn_re, turn_im = params[one][:, 0:1], params[one][:, 1:2]
            in_coeff, out_re, out_im = (params[one][:, at : at + 1] for at in (2, 3, 4))
            up_re, up_im, down_re, down_im, _, _ = tables[one]
            out_up_re = out_re * up_re - out_im * up_im
            out_up_im = out_re * up_im + out_im * up_re
            kernel_rows.append(jnp.sum(in_coeff * out_up_re, axis=0, keepdims=True))
            mixers.append(
                jnp.concatenate(
                    [
                        turn_re * out_up_re - turn_im * out_up_im,
                        -(turn_re * out_up_im + turn_im * out_up_re),
                    ],
                    axis=0,
                )
            )
            feed = jnp.concatenate([in_coeff * down_re, in_coeff * down_im], axis=0)
            ends.append(dot_split(halves(feed), series[one], NT))
        starts_row = start_row[...]
        held_re, held_im = state_scan(
            jnp.concatenate([part[:STATES] for part in ends], axis=0),
            jnp.concatenate([part[STATES:] for part in ends], axis=0),
            jnp.concatenate([part[4][:, :units] for part in tables], axis=0),
            jnp.concatenate([part[5][:, :units] for part in tables], axis=0),
            lambda lanes, distance: (lanes - distance) >= starts_row,
            units,
            1,
        )
        smoothed = []
        for one in many:
            span = slice(one * STATES, (one + 1) * STATES)
            held = jnp.concatenate([held_re[span], held_im[span]], axis=0)
            smoothed.append(
                dot_split(series[one], halves(toeplitz(kernel_rows[one])), NN)
                + dot_split(halves(held), halves(mixers[one]), TN)
            )
        for index in range(4):
            table_ref[index, pl.ds(base, BATCH * STATES), :] = jnp.concatenate(
                [part[index] for part in tables], axis=0
            )
        hold_ref[0, pl.ds(base, BATCH * STATES), :] = held_re
        hold_ref[1, pl.ds(base, BATCH * STATES), :] = held_im
        for one in many:
            row_ref[pl.ds(first + one, 1), :] = kernel_rows[one]
            ends_ref[pl.ds(first + one, units, stride=GS), :] = smoothed[one]
        return unused

    lax.fori_loop(0, GS // BATCH, first_pass, 0)
    for unit in range(units):
        here = slice(unit * GS, (unit + 1) * GS)
        normed = normed_ref[here, :]
        pre_act = ends_ref[here, :] + skip * normed
        pre_ref[0, here, :] = pre_act
        device, spot = places[unit]
        across = slice(spot * UNIT, (spot + 1) * UNIT)
        span = slice(unit * UNIT, (unit + 1) * UNIT)
        plain_ref[device, 0, :, across] = x_ref[:, span].astype(jnp.bfloat16)
        plain_ref[device, 1, :, across] = teacher_ref[:, span].astype(jnp.bfloat16)
        send_ref[device, 0, :, across] = normed.astype(jnp.bfloat16)
        send_ref[device, 1, :, across] = (pre_act * jax.nn.sigmoid(pre_act)).astype(jnp.bfloat16)


def front_backward_kernel(
    places,
    units,
    start_row,
    stop_row,
    start_col,
    stop_col,
    x_ref,
    state_ref,
    channel_ref,
    grad_ref,
    direct_ref,
    pre_ref,
    stat_ref,
    table_ref,
    row_ref,
    hold_ref,
    output_ref,
    out_ref,
    state_grad_ref,
    channel_grad_ref,
    normed_ref,
    slope_ref,
    back_ref,
    sums_ref,
):
    f32 = jnp.float32
    gain, bias, skip = channel_ref[:, 0:1], channel_ref[:, 1:2], channel_ref[:, 2:3]
    skip_sum = jnp.zeros((GS, UNIT), f32)
    for unit in range(units):
        here = slice(unit * GS, (unit + 1) * GS)
        device, spot = places[unit]
        across = slice(spot * UNIT, (spot + 1) * UNIT)
        tile = x_ref[:, unit * UNIT : (unit + 1) * UNIT]
        mean_row = stat_ref[0, unit : unit + 1, :]
        std_row = stat_ref[0, units + unit : units + unit + 1, :]
        normed = (tile - mean_row) * std_row * gain + bias
        normed_ref[here, :] = normed
        pre_act = pre_ref[0, here, :]
        logistic = jax.nn.sigmoid(pre_act)
        slope = (
            grad_ref[device, 1, :, across].astype(f32)
            * logistic
            * (1.0 + pre_act * (1.0 - logistic))
        )
        slope_ref[here, :] = slope
        skip_sum = skip_sum + slope * normed
    channel_grad_ref[:, 2:3] = jnp.sum(skip_sum, axis=1, keepdims=True)

    lag = lax.broadcasted_iota(jnp.int32, (STATES, UNIT), 1).astype(f32)

    def channel_pass(step, unused):
        first = step * BATCH_BACK
        many = range(BATCH_BACK)
        base = pl.multiple_of(first * STATES, BATCH_BACK * STATES)

        def pick(ref_at):
            return [ref_at[one * STATES : (one + 1) * STATES] for one in many]

        rows_here = pl.ds(base, BATCH_BACK * STATES)
        params = pick(state_ref[rows_here, :])
        up_re_all, up_im_all, down_re_all, down_im_all = (
            pick(table_ref[index, rows_here, :]) for index in range(4)
        )
        held_re_all, held_im_all = (pick(hold_ref[index, rows_here, :]) for index in range(2))
        kernel_rows = [row_ref[pl.ds(first + one, 1), :] for one in many]
        slopes = [halves(slope_ref[pl.ds(first + one, units, stride=GS), :]) for one in many]
        series = [halves(normed_ref[pl.ds(first + one, units, stride=GS), :]) for one in many]
        nexts, mixes, pulled = [], [], []
        for one in many:
            turn_re, turn_im = params[one][:, 0:1], params[one][:, 1:2]
            out_re, out_im = params[one][:, 3:4], params[one][:, 4:5]
            next_re = turn_re * up_re_all[one] - turn_im * up_im_all[one]
            next_im = turn_re * up_im_all[one] + turn_im * up_re_all[one]
            mix_re = out_re * next_re - out_im * next_im
            mix_im = out_re * next_im + out_im * next_re
            nexts.append((next_re, next_im))
            mixes.append((mix_re, mix_im))
            pulled.append(
                dot_split(halves(jnp.concatenate([mix_re, -mix_im], axis=0)), slopes[one], NT)
            )
        stops_row = stop_row[...]
        leaps_re = [jnp.broadcast_to(part[:, 5:6], (STATES, units)) for part in params]
        leaps_im = [jnp.broadcast_to(-part[:, 6:7], (STATES, units)) for part in params]
        pull_re_all, pull_im_all = state_scan(
            jnp.concatenate([part[:STATES] for part in pulled], axis=0),
            jnp.concatenate([part[STATES:] for part in pulled], axis=0),
            jnp.concatenate(leaps_re, axis=0),
            jnp.concatenate(leaps_im, axis=0),
            lambda lanes, distance: (lanes + distance) <= stops_row,
            units,
            -1,
        )
        pull_re_all, pull_im_all = pick(pull_re_all), pick(pull_im_all)
        backs, columns = [], []
        for one in many:
            in_coeff, out_re, out_im = (params[one][:, at : at + 1] for at in (2, 3, 4))
            leap_re, leap_im = params[one][:, 5:6], params[one][:, 6:7]
            up_re, up_im = up_re_all[one], up_im_all[one]
            down_re, down_im = down_re_all[one], down_im_all[one]
            (next_re, next_im), (mix_re, mix_im) = nexts[one], mixes[one]
            pull_re, pull_im = pull_re_all[one], pull_im_all[one]
            held_re, held_im = held_re_all[one], held_im_all[one]
            pull = halves(jnp.concatenate([pull_re, pull_im], axis=0))
            held = halves(jnp.concatenate([held_re, held_im], axis=0))
            feed_re, feed_im = in_coeff * down_re, in_coeff * down_im
            feed = halves(jnp.concatenate([feed_re, feed_im], axis=0))
            matrix = halves(toeplitz(kernel_rows[one]))
            backs.append(dot_split(slopes[one], matrix, NT) + dot_split(pull, feed, TN))
            lags = lag_sums(dot_split(slopes[one], reversed_lanes(series[one]), TN))
            mix_grad = dot_split(held, slopes[one], NN)
            feed_grad = dot_split(pull, series[one], NN)
            mg_re, mg_im = mix_grad[:STATES], -mix_grad[STATES:]
            fg_re, fg_im = feed_grad[:STATES], feed_grad[STATES:]
            leap_grad_re = held_re * pull_re + held_im * pull_im
            leap_grad_im = held_re * pull_im - held_im * pull_re
            leap_grad_re = jnp.sum(leap_grad_re, axis=1, keepdims=True)
            leap_grad_im = jnp.sum(leap_grad_im, axis=1, keepdims=True)
            lag_up_re, lag_up_im = lags * up_re, lags * up_im
            out_grad_re = jnp.sum(
                in_coeff * lag_up_re + mg_re * next_re + mg_im * next_im, axis=1, keepdims=True
            )
            out_grad_im = jnp.sum(
                -in_coeff * lag_up_im + mg_im * next_re - mg_re * next_im, axis=1, keepdims=True
            )
            tap_re = out_re * lag_up_re - out_im * lag_up_im
            tap_im = out_re * lag_up_im + out_im * lag_up_re
            in_grad = jnp.sum(tap_re + fg_re * down_re + fg_im * down_im, axis=1, keepdims=True)
            log_re = jnp.sum(
                lag * in_coeff * tap_re
                + (lag + 1.0) * (mix_re * mg_re + mix_im * mg_im)
                + (UNIT - 1.0 - lag) * (feed_re * fg_re + feed_im * fg_im),
                axis=1,
                keepdims=True,
            ) + UNIT * (leap_re * leap_grad_re + leap_im * leap_grad_im)
            log_im = jnp.sum(
                -lag * in_coeff * tap_im
                + (lag + 1.0) * (mix_re * mg_im - mix_im * mg_re)
                + (UNIT - 1.0 - lag) * (feed_re * fg_im - feed_im * fg_re),
                axis=1,
                keepdims=True,
            ) + UNIT * (leap_re * leap_grad_im - leap_im * leap_grad_re)
            columns.append((log_re, log_im, in_grad, out_grad_re, out_grad_im))
        for one in many:
            back_ref[pl.ds(first + one, units, stride=GS), :] = backs[one]
        for index in range(5):
            state_grad_ref[rows_here, index : index + 1] = jnp.concatenate(
                [part[index] for part in columns], axis=0
            )
        return unused

    lax.fori_loop(0, GS // BATCH_BACK, channel_pass, 0)

    gain_sum = jnp.zeros((GS, UNIT), f32)
    bias_sum = jnp.zeros((GS, UNIT), f32)
    for unit in range(units):
        here = slice(unit * GS, (unit + 1) * GS)
        device, spot = places[unit]
        across = slice(spot * UNIT, (spot + 1) * UNIT)
        tile = x_ref[:, unit * UNIT : (unit + 1) * UNIT]
        mean_row = stat_ref[0, unit : unit + 1, :]
        std_row = stat_ref[0, units + unit : units + unit + 1, :]
        plain = (tile - mean_row) * std_row
        total = (
            grad_ref[device, 0, :, across].astype(f32)
            + skip * slope_ref[here, :]
            + back_ref[here, :]
        )
        gain_sum = gain_sum + total * plain
        bias_sum = bias_sum + total
        scaled = total * gain
        back_ref[here, :] = scaled
        sums_ref[unit : unit + 1, :] = jnp.sum(scaled, axis=0, keepdims=True)
        sums_ref[units + unit : units + unit + 1, :] = jnp.sum(
            scaled * plain, axis=0, keepdims=True
        )
    channel_grad_ref[:, 0:1] = jnp.sum(gain_sum, axis=1, keepdims=True)
    channel_grad_ref[:, 1:2] = jnp.sum(bias_sum, axis=1, keepdims=True)
    mean_val, inv_std = stat_ref[0, :units, :], stat_ref[0, units:, :]
    var_grad = -0.5 * inv_std * inv_std * sums_ref[units:, :]
    mean_grad = -inv_std * sums_ref[:units, :] - 2.0 * mean_val * var_grad
    unit_at = lax.broadcasted_iota(jnp.int32, (units, UNIT), 0)
    lane_at = lax.broadcasted_iota(jnp.int32, (units, UNIT), 1)
    counted = (GS * ((unit_at - start_col[...]) * UNIT + lane_at + 1)).astype(f32)
    sums_ref[:units, :] = mean_grad / counted
    sums_ref[units:, :] = var_grad / counted
    rows = lax.broadcasted_iota(jnp.int32, (UNIT, UNIT), 0)
    lanes = lax.broadcasted_iota(jnp.int32, (UNIT, UNIT), 1)
    inside = dot_exact(sums_ref[...], (rows >= lanes).astype(f32))
    sooner = lax.broadcasted_iota(jnp.int32, (units, units), 0)
    later = lax.broadcasted_iota(jnp.int32, (units, units), 1)
    after = ((later > sooner) & (later <= stop_col[...])).astype(f32)
    totals = jnp.broadcast_to(inside[:, 0:1], (2 * units, UNIT))
    sums_ref[:units, :] = inside[:units] + dot_exact(after, totals[:units])
    sums_ref[units:, :] = 2.0 * (inside[units:] + dot_exact(after, totals[units:]))
    for unit in range(units):
        here = slice(unit * GS, (unit + 1) * GS)
        device, spot = places[unit]
        across = slice(spot * UNIT, (spot + 1) * UNIT)
        span = slice(unit * UNIT, (unit + 1) * UNIT)
        out_ref[:, span] = (
            back_ref[here, :] * stat_ref[0, units + unit : units + unit + 1, :]
            + sums_ref[unit : unit + 1, :]
            + x_ref[:, span] * sums_ref[units + unit : units + unit + 1, :]
            + direct_ref[device, 0, :, across].astype(f32)
        )
        output_ref[:, span] = direct_ref[device, 1, :, across].astype(f32)


def sequence_bounds(block_first, blocks, units):
    per_block = units // blocks
    index = jnp.arange(units, dtype=jnp.int32)
    begins = jnp.where(
        (index % per_block == 0) & (jnp.repeat(block_first, per_block) == 1), index, 0
    )
    starts = lax.cummax(begins)
    is_start = (index % per_block == 0) & (jnp.repeat(block_first, per_block) == 1)
    following = jnp.where(is_start, index - 1, units - 1)
    shifted = jnp.concatenate([following[1:], jnp.full((1,), units - 1, jnp.int32)])
    stops = lax.cummin(shifted, reverse=True)
    return starts, stops


def whole(shape):
    return pl.BlockSpec(shape, lambda group: (0,) * len(shape))


def front_forward(layer_input, teacher, state_params, channel_params, bounds, places, devices):
    channels, slots = layer_input.shape
    units = slots // UNIT
    tokens = slots // devices
    groups = channels // GS
    starts, stops = bounds
    f32 = jnp.float32
    return pl.pallas_call(
        partial(front_forward_kernel, places, units),
        grid=(groups,),
        in_specs=[
            whole((1, units)),
            whole((units, 1)),
            pl.BlockSpec((GS, slots), lambda group: (group, 0)),
            pl.BlockSpec((GS, slots), lambda group: (group, 0)),
            pl.BlockSpec((GS * STATES, 8), lambda group: (group, 0)),
            pl.BlockSpec((GS, 8), lambda group: (group, 0)),
        ],
        out_specs=[
            pl.BlockSpec((devices, 2, GS, tokens), lambda group: (0, 0, group, 0)),
            pl.BlockSpec((devices, 2, GS, tokens), lambda group: (0, 0, group, 0)),
            pl.BlockSpec((1, units * GS, UNIT), lambda group: (group, 0, 0)),
            pl.BlockSpec((1, 2 * units, UNIT), lambda group: (group, 0, 0)),
            pl.BlockSpec((4, GS * STATES, UNIT), lambda group: (0, group, 0)),
            pl.BlockSpec((GS, UNIT), lambda group: (group, 0)),
            pl.BlockSpec((2, GS * STATES, units), lambda group: (0, group, 0)),
        ],
        out_shape=[
            jax.ShapeDtypeStruct((devices, 2, channels, tokens), jnp.bfloat16),
            jax.ShapeDtypeStruct((devices, 2, channels, tokens), jnp.bfloat16),
            jax.ShapeDtypeStruct((groups, units * GS, UNIT), f32),
            jax.ShapeDtypeStruct((groups, 2 * units, UNIT), f32),
            jax.ShapeDtypeStruct((4, channels * STATES, UNIT), f32),
            jax.ShapeDtypeStruct((channels, UNIT), f32),
            jax.ShapeDtypeStruct((2, channels * STATES, units), f32),
        ],
        scratch_shapes=[
            pltpu.VMEM((units * GS, UNIT), f32),
            pltpu.VMEM((2 * units, UNIT), f32),
            pltpu.VMEM((units * GS, UNIT), f32),
        ],
        cost_estimate=pl.CostEstimate(
            flops=channels * slots * 60000, bytes_accessed=channels * slots * 24, transcendentals=0
        ),
        name="front_forward",
    )(starts[None, :], starts[:, None], layer_input, teacher, state_params, channel_params)


def front_backward(
    layer_input, state_params, channel_params, bounds, places, devices, grads, direct, saved
):
    channels, slots = layer_input.shape
    units = slots // UNIT
    tokens = slots // devices
    groups = channels // GS
    starts, stops = bounds
    f32 = jnp.float32
    return pl.pallas_call(
        partial(front_backward_kernel, places, units),
        grid=(groups,),
        in_specs=[
            whole((1, units)),
            whole((1, units)),
            whole((units, 1)),
            whole((units, 1)),
            pl.BlockSpec((GS, slots), lambda group: (group, 0)),
            pl.BlockSpec((GS * STATES, 8), lambda group: (group, 0)),
            pl.BlockSpec((GS, 8), lambda group: (group, 0)),
            pl.BlockSpec((devices, 2, GS, tokens), lambda group: (0, 0, group, 0)),
            pl.BlockSpec((devices, 2, GS, tokens), lambda group: (0, 0, group, 0)),
            pl.BlockSpec((1, units * GS, UNIT), lambda group: (group, 0, 0)),
            pl.BlockSpec((1, 2 * units, UNIT), lambda group: (group, 0, 0)),
            pl.BlockSpec((4, GS * STATES, UNIT), lambda group: (0, group, 0)),
            pl.BlockSpec((GS, UNIT), lambda group: (group, 0)),
            pl.BlockSpec((2, GS * STATES, units), lambda group: (0, group, 0)),
        ],
        out_specs=[
            pl.BlockSpec((GS, slots), lambda group: (group, 0)),
            pl.BlockSpec((GS, slots), lambda group: (group, 0)),
            pl.BlockSpec((GS * STATES, 8), lambda group: (group, 0)),
            pl.BlockSpec((GS, 8), lambda group: (group, 0)),
        ],
        out_shape=[
            jax.ShapeDtypeStruct((channels, slots), f32),
            jax.ShapeDtypeStruct((channels, slots), f32),
            jax.ShapeDtypeStruct((channels * STATES, 8), f32),
            jax.ShapeDtypeStruct((channels, 8), f32),
        ],
        scratch_shapes=[
            pltpu.VMEM((units * GS, UNIT), f32),
            pltpu.VMEM((units * GS, UNIT), f32),
            pltpu.VMEM((units * GS, UNIT), f32),
            pltpu.VMEM((2 * units, UNIT), f32),
        ],
        cost_estimate=pl.CostEstimate(
            flops=channels * slots * 140000, bytes_accessed=channels * slots * 32, transcendentals=0
        ),
        name="front_backward",
    )(
        starts[None, :],
        stops[None, :],
        starts[:, None],
        stops[:, None],
        layer_input,
        state_params,
        channel_params,
        grads,
        direct,
        *saved,
    )


def front_parameters(rate, angle, ema_in, out_re, out_im, gain, bias, skip):
    magnitude = 1.0 - rate
    leap = jnp.exp(UNIT * jnp.log(magnitude))
    columns = [
        magnitude * jnp.cos(angle),
        magnitude * jnp.sin(angle),
        jnp.sqrt(2.0 * rate) * ema_in,
        out_re,
        out_im,
        leap * jnp.cos(UNIT * angle),
        leap * jnp.sin(UNIT * angle),
        rate,
    ]
    states = jnp.stack(columns, axis=-1).reshape(-1, 8)
    channels = jnp.stack([gain, bias, skip] + [skip] * 5, axis=-1)
    return states, channels


def front_parameter_grads(state_grads, channel_grads, rate, ema_in):
    shaped = state_grads.reshape(rate.shape + (8,))
    log_re, log_im, in_grad = shaped[..., 0], shaped[..., 1], shaped[..., 2]
    root = jnp.sqrt(2.0 * rate)
    return (
        channel_grads[:, 0],
        channel_grads[:, 1],
        in_grad * ema_in / root - log_re / (1.0 - rate),
        log_im,
        in_grad * root,
        shaped[..., 3],
        shaped[..., 4],
        channel_grads[:, 2],
    )


def unit_places(slots, devices, blocks):
    units = slots // UNIT
    per_block = units // blocks
    group = devices // blocks
    per_device = per_block // group
    places = [None] * units
    for block in range(blocks):
        for member in range(group):
            if per_device % 2 == 0:
                half = per_device // 2
                mirror = 2 * group - 1 - member
                owned = [member * half + step for step in range(half)]
                owned += [mirror * half + step for step in range(half)]
            else:
                owned = [member * per_device + step for step in range(per_device)]
            for spot, unit in enumerate(owned):
                places[block * per_block + unit] = (block * group + member, spot)
    return places


def chunk_sites(group, tokens):
    if tokens % (2 * UNIT) == 0:
        half = tokens // 2
        sites = [(member, 0) for member in range(group)]
        sites += [(2 * group - 1 - chunk, half) for chunk in range(group, 2 * group)]
        return half, sites
    return tokens, [(member, 0) for member in range(group)]


def query_pieces(group, tokens, member):
    half, sites = chunk_sites(group, tokens)
    if half < tokens:
        return half, [(member, 0), (2 * group - 1 - member, half)]
    return half, [(member, 0)]


def masked_scores(turned, keys, allowed, scale):
    products = lax.dot_general(turned, keys, NN, preferred_element_type=jnp.float32) * scale
    return jnp.where(allowed, products, NEGATIVE)


def causal_tile(size, key_chunk, query_chunk):
    rows = lax.broadcasted_iota(jnp.int32, (size, size), 0)
    lanes = lax.broadcasted_iota(jnp.int32, (size, size), 1)
    return (lanes <= rows) | (key_chunk < query_chunk)


def attention_forward_kernel(
    group, member_ref, query_ref, keep_ref, out_ref, log_ref, score_ref, prob_ref
):
    f32, bf16 = jnp.float32, jnp.bfloat16
    tokens = query_ref.shape[1]
    width = out_ref.shape[0]
    member = member_ref[0]
    half, pieces = query_pieces(group, tokens, member)
    _, sites = chunk_sites(group, tokens)
    scale = Z ** (-0.5)
    for chunk, offset in pieces:
        turned = query_ref[:, offset : offset + half].astype(f32).T.astype(bf16)
        log_ref[offset : offset + half, :] = jnp.full((half, UNIT), NEGATIVE, f32)
        out_ref[:, offset : offset + half] = jnp.zeros((width, half), f32)
        for index, (owner, start) in enumerate(sites):

            @pl.when(index <= chunk)
            def _():
                keys = keep_ref[owner, width:, start : start + half]
                scores = masked_scores(turned, keys, causal_tile(half, index, chunk), scale)
                score_ref[index] = scores
                log_ref[offset : offset + half, :] = jnp.maximum(
                    log_ref[offset : offset + half, :], jnp.max(scores, axis=1, keepdims=True)
                )

        tops = log_ref[offset : offset + half, 0:1]
        prob_ref[:, 0:1] = jnp.zeros((half, 1), f32)
        for index in range(len(sites)):

            @pl.when(index <= chunk)
            def _():
                exponent = jnp.exp(score_ref[index] - tops)
                score_ref[index] = exponent
                prob_ref[:, 0:1] += jnp.sum(exponent, axis=1, keepdims=True)

        totals = prob_ref[:, 0:1]
        log_ref[offset : offset + half, :] = jnp.broadcast_to(
            tops + jnp.log(totals), (half, UNIT)
        )
        for index, (owner, start) in enumerate(sites):

            @pl.when(index <= chunk)
            def _():
                probs = (score_ref[index] / totals).astype(bf16)
                values = keep_ref[owner, :width, start : start + half]
                out_ref[:, offset : offset + half] += lax.dot_general(
                    values, probs, NT, preferred_element_type=f32
                )


def attention_backward_kernel(
    group,
    member_ref,
    query_ref,
    keep_ref,
    grad_ref,
    log_ref,
    query_grad_ref,
    out_ref,
    prob_ref,
    slope_ref,
    low_ref,
    score_grad_ref,
    dot_ref,
    turned_ref,
):
    f32, bf16 = jnp.float32, jnp.bfloat16
    tokens = query_ref.shape[1]
    width = grad_ref.shape[0]
    member = member_ref[0]
    half, pieces = query_pieces(group, tokens, member)
    _, sites = chunk_sites(group, tokens)
    scale = Z ** (-0.5)
    for which, (chunk, offset) in enumerate(pieces):
        here = slice(offset, offset + half)
        turned = query_ref[:, here].astype(f32).T.astype(bf16)
        for start in range(0, width, half):
            turned_ref[:, start : start + half] = (
                grad_ref[start : start + half, here].astype(f32).T.astype(bf16)
            )
        logs = log_ref[here, 0:1]
        dot_ref[...] = jnp.zeros(dot_ref.shape, f32)
        query_grad_ref[:, here] = jnp.zeros((Z, half), f32)
        for index, (owner, start) in enumerate(sites):

            @pl.when(index <= chunk)
            def _():
                keys = keep_ref[owner, width:, start : start + half]
                scores = masked_scores(turned, keys, causal_tile(half, index, chunk), scale)
                probs = jnp.exp(scores - logs)
                prob_ref[index] = probs
                low_ref[which, index] = probs.astype(bf16)
                slope = lax.dot_general(
                    turned_ref[...],
                    keep_ref[owner, :width, start : start + half],
                    NN,
                    preferred_element_type=f32,
                )
                slope_ref[index] = slope
                dot_ref[:, 0:1] += jnp.sum(probs * slope, axis=1, keepdims=True)

        dots = dot_ref[:, 0:1]
        for index, (owner, start) in enumerate(sites):

            @pl.when(index <= chunk)
            def _():
                score_grad = (prob_ref[index] * (slope_ref[index] - dots)).astype(bf16)
                score_grad_ref[which, index] = score_grad
                keys = keep_ref[owner, width:, start : start + half]
                query_grad_ref[:, here] += (
                    lax.dot_general(keys, score_grad, NT, preferred_element_type=f32) * scale
                )

    last = pieces[-1]
    for index, (owner, start) in enumerate(sites):
        there = slice(start, start + half)

        def emit(used):
            value_sum, key_sum = None, None
            for which in used:
                offset = pieces[which][1]
                here = slice(offset, offset + half)
                value_part = lax.dot_general(
                    grad_ref[:, here], low_ref[which, index], NN, preferred_element_type=f32
                )
                key_part = lax.dot_general(
                    query_ref[:, here], score_grad_ref[which, index], NN, preferred_element_type=f32
                )
                value_sum = value_part if value_sum is None else value_sum + value_part
                key_sum = key_part if key_sum is None else key_sum + key_part
            out_ref[owner, :width, there] = value_sum.astype(bf16)
            out_ref[owner, width:, there] = (key_sum * scale).astype(bf16)

        if len(pieces) == 2:

            @pl.when(index <= pieces[0][0])
            def _():
                emit((0, 1))

            @pl.when((index > pieces[0][0]) & (index <= last[0]))
            def _():
                emit((1,))

        else:

            @pl.when(index <= last[0])
            def _():
                emit((0,))

        @pl.when(index > last[0])
        def _():
            out_ref[owner, :, there] = jnp.zeros((out_ref.shape[1], half), bf16)


VMEM_BUDGET = 60 * 1024 * 1024


def attention_forward(member, queries, key_values, group):
    tokens = queries.shape[1]
    width = key_values.shape[1] - queries.shape[0]
    half, sites = chunk_sites(group, tokens)
    f32 = jnp.float32
    vmem = pl.BlockSpec(memory_space=pltpu.VMEM)
    return pl.pallas_call(
        partial(attention_forward_kernel, group),
        in_specs=[pl.BlockSpec(memory_space=pltpu.SMEM), vmem, vmem],
        out_specs=[vmem, vmem],
        out_shape=[
            jax.ShapeDtypeStruct((width, tokens), f32),
            jax.ShapeDtypeStruct((tokens, UNIT), f32),
        ],
        scratch_shapes=[
            pltpu.VMEM((len(sites), half, half), f32),
            pltpu.VMEM((half, UNIT), f32),
        ],
        compiler_params=pltpu.CompilerParams(vmem_limit_bytes=VMEM_BUDGET),
        cost_estimate=pl.CostEstimate(
            flops=2 * tokens * tokens * group * (width + Z),
            bytes_accessed=2 * key_values.size + 4 * width * tokens,
            transcendentals=tokens * tokens * group,
        ),
        name="attention_forward",
    )(member, queries, key_values)


def attention_backward(member, queries, key_values, grads, logs, group):
    tokens = queries.shape[1]
    half, sites = chunk_sites(group, tokens)
    count = tokens // half
    f32, bf16 = jnp.float32, jnp.bfloat16
    vmem = pl.BlockSpec(memory_space=pltpu.VMEM)
    return pl.pallas_call(
        partial(attention_backward_kernel, group),
        in_specs=[pl.BlockSpec(memory_space=pltpu.SMEM), vmem, vmem, vmem, vmem],
        out_specs=[vmem, vmem],
        out_shape=[
            jax.ShapeDtypeStruct(queries.shape, f32),
            jax.ShapeDtypeStruct(key_values.shape, bf16),
        ],
        scratch_shapes=[
            pltpu.VMEM((len(sites), half, half), f32),
            pltpu.VMEM((len(sites), half, half), f32),
            pltpu.VMEM((count, len(sites), half, half), bf16),
            pltpu.VMEM((count, len(sites), half, half), bf16),
            pltpu.VMEM((half, UNIT), f32),
            pltpu.VMEM((half, grads.shape[0]), bf16),
        ],
        compiler_params=pltpu.CompilerParams(vmem_limit_bytes=VMEM_BUDGET),
        cost_estimate=pl.CostEstimate(
            flops=4 * tokens * tokens * group * (grads.shape[0] + Z),
            bytes_accessed=4 * key_values.size,
            transcendentals=tokens * tokens * group,
        ),
        name="attention_backward",
    )(member, queries, key_values, grads, logs)


PIECES = 4


def meet_neighbours(side, across):
    barrier = pltpu.get_barrier_semaphore()
    for target in (side, across):
        pl.semaphore_signal(
            barrier, inc=1, device_id={"col": target}, device_id_type=pl.DeviceIdType.MESH
        )
    pl.semaphore_wait(barrier, 2)


def neighbours():
    me = lax.axis_index("col")
    return me, me + 1 - 2 * (me % 2), (me + 2) % 4


def push(source, target, send_sem, recv_sem, device):
    return pltpu.make_async_remote_copy(
        src_ref=source,
        dst_ref=target,
        send_sem=send_sem,
        recv_sem=recv_sem,
        device_id={"col": device},
        device_id_type=pl.DeviceIdType.MESH,
    )


def gather_kernel(
    own_ref, out_ref, local_sem, cross_send, cross_recv, side_send, side_recv, pass_send, pass_recv
):
    me, side, across = neighbours()
    count = own_ref.shape[0] // PIECES
    meet_neighbours(side, across)
    crossing = []
    for piece in range(PIECES):
        rows = pl.ds(piece * count, count)
        copy = push(
            own_ref.at[rows],
            out_ref.at[me, rows],
            cross_send.at[piece],
            cross_recv.at[piece],
            across,
        )
        copy.start()
        crossing.append(copy)
    beside = push(own_ref, out_ref.at[me], side_send, side_recv, side)
    beside.start()
    local = pltpu.make_async_copy(own_ref, out_ref.at[me], local_sem)
    local.start()
    passing = []
    for piece in range(PIECES):
        rows = pl.ds(piece * count, count)
        crossing[piece].wait_recv()
        copy = push(
            out_ref.at[across, rows],
            out_ref.at[across, rows],
            pass_send.at[piece],
            pass_recv.at[piece],
            side,
        )
        copy.start()
        passing.append(copy)
    for piece in range(PIECES):
        crossing[piece].wait_send()
        passing[piece].wait()
    beside.wait()
    local.wait()


def gather_members(own):
    dma = pltpu.SemaphoreType.DMA
    anywhere = pl.BlockSpec(memory_space=pl.ANY)
    return pl.pallas_call(
        gather_kernel,
        in_specs=[anywhere],
        out_specs=anywhere,
        out_shape=jax.ShapeDtypeStruct((4,) + own.shape, own.dtype),
        scratch_shapes=[
            dma,
            dma((PIECES,)),
            dma((PIECES,)),
            dma,
            dma,
            dma((PIECES,)),
            dma((PIECES,)),
        ],
        compiler_params=pltpu.CompilerParams(collective_id=0, has_side_effects=True),
        name="gather_members",
    )(own)


def reduce_kernel(
    parts_ref,
    out_ref,
    beside_ref,
    sum_ref,
    landed_ref,
    first_send,
    first_recv,
    second_send,
    second_recv,
    cross_send,
    cross_recv,
):
    f32, bf16 = jnp.float32, jnp.bfloat16
    me, side, across = neighbours()
    count = out_ref.shape[0] // PIECES
    beyond = (side + 2) % 4
    meet_neighbours(side, across)
    first, second, crossing = [], [], []
    for piece in range(PIECES):
        rows = pl.ds(piece * count, count)
        copy = push(
            parts_ref.at[beyond, rows],
            beside_ref.at[0, rows],
            first_send.at[piece],
            first_recv.at[piece],
            side,
        )
        copy.start()
        first.append(copy)
    for piece in range(PIECES):
        rows = pl.ds(piece * count, count)
        copy = push(
            parts_ref.at[side, rows],
            beside_ref.at[1, rows],
            second_send.at[piece],
            second_recv.at[piece],
            side,
        )
        copy.start()
        second.append(copy)
    for piece in range(PIECES):
        rows = pl.ds(piece * count, count)
        first[piece].wait_recv()
        total = parts_ref[across, rows, :].astype(f32) + beside_ref[0, rows, :].astype(f32)
        sum_ref[rows, :] = total.astype(bf16)
        copy = push(
            sum_ref.at[rows],
            landed_ref.at[rows],
            cross_send.at[piece],
            cross_recv.at[piece],
            across,
        )
        copy.start()
        crossing.append(copy)
    for piece in range(PIECES):
        rows = pl.ds(piece * count, count)
        second[piece].wait_recv()
        crossing[piece].wait_recv()
        out_ref[rows, :] = (
            parts_ref[me, rows, :].astype(f32)
            + beside_ref[1, rows, :].astype(f32)
            + landed_ref[rows, :].astype(f32)
        )
    for piece in range(PIECES):
        first[piece].wait_send()
        second[piece].wait_send()
        crossing[piece].wait_send()


def reduce_members(parts):
    dma = pltpu.SemaphoreType.DMA
    vmem = pl.BlockSpec(memory_space=pltpu.VMEM)
    shape = parts.shape[1:]
    return pl.pallas_call(
        reduce_kernel,
        in_specs=[vmem],
        out_specs=vmem,
        out_shape=jax.ShapeDtypeStruct(shape, jnp.float32),
        scratch_shapes=[
            pltpu.VMEM((2,) + shape, parts.dtype),
            pltpu.VMEM(shape, parts.dtype),
            pltpu.VMEM(shape, parts.dtype),
        ]
        + [dma((PIECES,))] * 6,
        compiler_params=pltpu.CompilerParams(
            collective_id=1, has_side_effects=True, vmem_limit_bytes=VMEM_BUDGET
        ),
        name="reduce_members",
    )(parts)


def silu_slope(pre_act):
    logistic = jax.nn.sigmoid(pre_act)
    return logistic * (1.0 + pre_act * (1.0 - logistic))


def contract_first(left_in, right_in):
    return lax.dot_general(
        left_in, right_in, (((0,), (0,)), ((), ())), preferred_element_type=jnp.float32
    )


def contract_last(left_in, right_in):
    return lax.dot_general(
        left_in, right_in, (((1,), (1,)), ((), ())), preferred_element_type=jnp.float32
    )


def silu(pre_act):
    return pre_act * jax.nn.sigmoid(pre_act)


def swap_blocks(array_in, outer, inner):
    shaped = array_in.reshape(outer, inner, -1, array_in.shape[-1])
    return shaped.transpose(1, 0, 2, 3).reshape(array_in.shape)


def project(weights, source):
    return jnp.concatenate(
        [contract_first(weights[part], source) for part in range(weights.shape[0])], axis=0
    )


def project_back(weights, grads):
    parts = weights.shape[0]
    pieces = grads.reshape(parts, -1, grads.shape[-1])
    total = None
    for part in range(parts):
        product = jnp.dot(weights[part], pieces[part], preferred_element_type=jnp.float32)
        total = product if total is None else total + product
    return total


def weight_products(source, grads, parts):
    pieces = grads.reshape(parts, -1, grads.shape[-1])
    return [contract_last(source, pieces[part]).astype(jnp.bfloat16) for part in range(parts)]


def shards(
    layer_input,
    teacher,
    block_len,
    block_first,
    norm_gain,
    norm_bias,
    ema_rate,
    ema_angle,
    ema_input,
    ema_out_real,
    ema_out_imag,
    ema_skip,
    w_value,
    w_shared,
    w_reset,
    w_hidden,
    w_update,
    query_gain,
    query_bias,
    key_gain,
    w_output,
    final_gain,
    final_bias,
    w_gate,
    w_up,
    w_down,
):
    bf16 = jnp.bfloat16
    grid = ("row", "col")
    rows, cols, dps = lax.axis_size("row"), lax.axis_size("col"), lax.axis_size("dp")
    devices = rows * cols
    slot_count = layer_input.shape[1]
    blocks_here = slot_count // SPAN
    group = devices // blocks_here
    tokens = slot_count // devices
    place = lax.axis_index("row") * cols + lax.axis_index("col")
    my_block = place // group
    member = place % group
    places = unit_places(slot_count, devices, blocks_here)
    state_params, channel_params = front_parameters(
        ema_rate,
        ema_angle,
        ema_input,
        ema_out_real,
        ema_out_imag,
        norm_gain,
        norm_bias,
        ema_skip,
    )
    bounds = sequence_bounds(block_first, blocks_here, slot_count // UNIT)

    def exchange(array_in):
        return lax.all_to_all(array_in, grid, 0, 0, tiled=True)

    def gather_weights(local):
        gathered = lax.all_gather(local, grid, axis=0)
        return gathered.reshape(rows, -1, local.shape[-1])

    def local_matrix(weight_list):
        flat = [weight.reshape(-1, weight.shape[-1]) for weight in weight_list]
        return flat[0] if len(flat) == 1 else jnp.concatenate(flat, axis=1)

    barrier = lax.optimization_barrier
    vectors = exchange(
        jnp.broadcast_to(
            jnp.concatenate([final_gain, final_bias, query_gain, query_bias, key_gain])[None],
            (devices, 2 * final_gain.shape[0] + 3 * query_gain.shape[0]),
        )
    )
    valid_here = jnp.sum(block_len).astype(jnp.float32)
    valid_all = lax.psum(jnp.broadcast_to(valid_here, (COUNT_ROWS, D)), "dp")
    valid_total = valid_all[0, 0]
    parts_out = w_output.shape[2] // w_value.shape[2]
    output_local = w_output.reshape(rows, parts_out, w_value.shape[2], -1)
    output_local = [output_local[:, part].reshape(-1, w_output.shape[-1]) for part in range(parts_out)]
    value_weights = gather_weights(local_matrix([w_value, w_shared]))
    rest_weights = gather_weights(
        jnp.concatenate(output_local + [local_matrix([w_reset, w_hidden, w_update])], axis=1)
    )
    inner_weights = gather_weights(local_matrix([w_gate, w_up]))
    down_weights = gather_weights(local_matrix([w_down]))
    feat_share, z_share = final_gain.shape[0], query_gain.shape[0]

    def whole_vector(start, share):
        return vectors[:, start : start + share].reshape(-1)

    gain_all = whole_vector(0, feat_share)
    bias_all = whole_vector(feat_share, feat_share)
    query_gain_all = whole_vector(2 * feat_share, z_share)
    query_bias_all = whole_vector(2 * feat_share + z_share, z_share)
    key_gain_all = whole_vector(2 * feat_share + 2 * z_share, z_share)

    half, pieces = query_pieces(group, tokens, member)
    positions = jnp.concatenate([chunk * half + jnp.arange(half) for chunk, offset in pieces])
    valid_mask = (positions < block_len[my_block]).astype(jnp.float32)

    send, send_plain, *saved = front_forward(
        layer_input, teacher, state_params, channel_params, bounds, places, devices
    )
    sources = exchange(send)
    feats = layer_input.shape[0]
    sources = sources.reshape(rows, cols, 2, feats, tokens).transpose(2, 1, 0, 3, 4)
    sources = sources.reshape(2, devices * feats, tokens)
    normed_low, mixed_low = sources[0], sources[1]
    n_value, n_shared, n_reset, n_hidden = (
        weight.shape[-1] for weight in (w_value, w_shared, w_reset, w_hidden)
    )
    n_out = w_output.shape[-1]
    skip_out = parts_out * n_out
    value_pre = project(value_weights[:, :, :n_value], normed_low)
    shared = project(value_weights[:, :, n_value:], mixed_low)
    mixed_out = [
        contract_first(rest_weights[part, :, skip_out:], mixed_low) for part in range(rows)
    ]

    def mixed_slice(start, count):
        return jnp.concatenate([piece[start : start + count] for piece in mixed_out], axis=0)

    reset_pre = mixed_slice(0, n_reset)
    hidden_pre = mixed_slice(n_reset, n_hidden)
    update_pre = mixed_slice(n_reset + n_hidden, n_hidden)
    values_low = silu(value_pre).astype(bf16)
    queries = (shared * query_gain_all[:, None] + query_bias_all[:, None]).astype(bf16)
    keys_low = (shared * key_gain_all[:, None]).astype(bf16)
    key_values = jnp.concatenate([values_low, keys_low], axis=0)
    near = rows == blocks_here and cols == 4
    if near:
        gathered_kv = gather_members(key_values)
    else:
        gathered_kv = lax.dynamic_slice_in_dim(
            lax.all_gather(key_values, grid, axis=0), my_block * group, group, 0
        )
    width = values_low.shape[0]
    send_plain, gathered_kv = barrier((send_plain, gathered_kv))
    plain = exchange(send_plain)
    plain = plain.astype(jnp.float32)
    input_slots = plain[:, 0].reshape(devices * feats, tokens)
    teacher_slots = plain[:, 1].reshape(devices * feats, tokens)

    attended, logs = attention_forward(member[None], queries, gathered_kv, group)
    reset_act = silu(reset_pre)
    att_in = (attended * reset_act).astype(bf16)
    att_in = att_in.reshape(rows, cols, parts_out, -1, tokens).transpose(2, 1, 0, 3, 4)
    att_in = att_in.reshape(parts_out, -1, tokens)
    summed = hidden_pre
    for part in range(parts_out):
        summed = summed + project(
            rest_weights[:, :, part * n_out : (part + 1) * n_out], att_in[part]
        )
    hidden_act = silu(summed)
    gate_act = jax.nn.sigmoid(update_pre)
    first_out = input_slots + gate_act * (hidden_act - input_slots)
    mean_val = jnp.mean(first_out, axis=0)
    inv_std = lax.rsqrt(jnp.mean(first_out * first_out, axis=0) - mean_val * mean_val + EPSILON)
    unit_norm = (first_out - mean_val) * inv_std
    final_norm = swap_blocks(
        (unit_norm * gain_all[:, None] + bias_all[:, None]).astype(bf16), rows, cols
    )
    n_inner = w_gate.shape[-1]
    inner_out = [contract_first(inner_weights[part], final_norm) for part in range(rows)]
    gate_pre = jnp.concatenate([piece[:n_inner] for piece in inner_out], axis=0)
    up_pre = jnp.concatenate([piece[n_inner:] for piece in inner_out], axis=0)
    inner_act = swap_blocks((silu(gate_pre) * up_pre).astype(bf16), rows, cols)
    output_slots = first_out + project(down_weights, inner_act)
    out_error = (output_slots - teacher_slots) * valid_mask
    loss_part = jnp.sum(out_error * out_error)
    out_grad = out_error * (slot_count * dps / valid_total)

    out_low = out_grad.astype(bf16)
    inner_grad = swap_blocks(project_back(down_weights, out_low), cols, rows)
    gate_grad = (inner_grad * up_pre * silu_slope(gate_pre)).astype(bf16)
    up_grad = (inner_grad * silu(gate_pre)).astype(bf16)
    inner_grads = jnp.concatenate(
        [gate_grad.reshape(rows, -1, tokens), up_grad.reshape(rows, -1, tokens)], axis=1
    )
    norm_grad = swap_blocks(
        project_back(inner_weights, inner_grads.reshape(-1, tokens)), cols, rows
    )

    def scatter_weight(product_list, rank):
        stacked = jnp.stack(product_list)
        shaped = stacked.reshape(devices, rows * rank, stacked.shape[-1])
        return lax.psum_scatter(shaped, grid, scatter_dimension=0, tiled=True)[0]

    down_sum = scatter_weight(weight_products(inner_act, out_low, rows), w_down.shape[2])
    inner_sum = scatter_weight(weight_products(final_norm, inner_grads, rows), w_gate.shape[2])
    down_sum, inner_sum, valid_all = barrier((down_sum, inner_sum, valid_all))
    down_sum, inner_sum = lax.psum((down_sum, inner_sum), "dp")

    final_gain_part = jnp.sum(norm_grad * unit_norm, axis=1)
    final_bias_part = jnp.sum(norm_grad, axis=1)
    unit_grad = norm_grad * gain_all[:, None]
    first_grad = out_grad + inv_std * (
        unit_grad
        - jnp.mean(unit_grad, axis=0)
        - unit_norm * jnp.mean(unit_grad * unit_norm, axis=0)
    )
    direct = exchange(
        jnp.stack(
            [
                (first_grad * (1.0 - gate_act)).reshape(devices, feats, tokens),
                output_slots.reshape(devices, feats, tokens),
            ],
            axis=1,
        ).astype(bf16)
    )
    update_grad = (first_grad * (hidden_act - input_slots) * gate_act * (1.0 - gate_act)).astype(
        bf16
    )
    summed_grad = (first_grad * gate_act * silu_slope(summed)).astype(bf16)
    att_grad = jnp.stack(
        [
            project_back(rest_weights[:, :, part * n_out : (part + 1) * n_out], summed_grad)
            for part in range(parts_out)
        ]
    )
    att_grad = att_grad.reshape(parts_out, cols, rows, feats, tokens).transpose(2, 1, 0, 3, 4)
    att_grad = att_grad.reshape(-1, tokens)
    attended_grad = (att_grad * reset_act).astype(bf16)
    reset_grad = (att_grad * attended * silu_slope(reset_pre)).astype(bf16)
    mixed_grads = jnp.concatenate(
        [piece.reshape(rows, -1, tokens) for piece in (reset_grad, summed_grad, update_grad)],
        axis=1,
    )
    rest_products = [
        jnp.concatenate(columns, axis=1)
        for columns in zip(
            *[weight_products(att_in[part], summed_grad, rows) for part in range(parts_out)],
            weight_products(mixed_low, mixed_grads, rows),
        )
    ]
    query_grad, kv_parts = attention_backward(
        member[None], queries, gathered_kv, attended_grad, logs, group
    )
    kv_parts, direct = barrier((kv_parts, direct))
    if near:
        kv_grads = reduce_members(kv_parts)
    else:
        spread = lax.dynamic_update_slice_in_dim(
            jnp.zeros((devices,) + kv_parts.shape[1:], bf16), kv_parts, my_block * group, 0
        )
        kv_grads = lax.psum_scatter(spread, grid, scatter_dimension=0, tiled=True)[0]
    kv_grads, rest_products = barrier((kv_grads, rest_products))
    rest_sum = scatter_weight(rest_products, w_value.shape[2])
    rest_sum, down_sum, inner_sum = barrier((rest_sum, down_sum, inner_sum))
    rest_sum = lax.psum(rest_sum, "dp")
    value_grad, key_grad = kv_grads[:width].astype(jnp.float32), kv_grads[width:].astype(jnp.float32)
    value_pre_grad = (value_grad * silu_slope(value_pre)).astype(bf16)
    shared_grad = (
        query_grad * query_gain_all[:, None] + key_grad * key_gain_all[:, None]
    ).astype(bf16)
    query_gain_part = jnp.sum(query_grad * shared, axis=1)
    query_bias_part = jnp.sum(query_grad, axis=1)
    key_gain_part = jnp.sum(key_grad * shared, axis=1)
    normed_back = project_back(value_weights[:, :, :n_value], value_pre_grad)
    mixed_back = project_back(
        rest_weights[:, :, skip_out:], mixed_grads.reshape(-1, tokens)
    ) + project_back(value_weights[:, :, n_value:], shared_grad)
    backs = jnp.stack([normed_back, mixed_back]).astype(bf16)
    backs = backs.reshape(2, cols, rows, feats, tokens).transpose(2, 1, 0, 3, 4)
    backs = exchange(backs.reshape(devices, 2, feats, tokens))
    layer_output, input_grad, state_grads, channel_grads = front_backward(
        layer_input, state_params, channel_params, bounds, places, devices, backs, direct, saved
    )
    param_grads = front_parameter_grads(state_grads, channel_grads, ema_rate, ema_input)

    value_products = [
        jnp.concatenate(pair, axis=1)
        for pair in zip(
            weight_products(normed_low, value_pre_grad, rows),
            weight_products(mixed_low, shared_grad, rows),
        )
    ]
    value_sum = scatter_weight(value_products, w_value.shape[2])
    value_sum, rest_sum = barrier((value_sum, rest_sum))
    value_sum = lax.psum(value_sum, "dp")

    vector_parts = [final_gain_part, final_bias_part, query_gain_part, query_bias_part, key_gain_part]
    vector_parts = jnp.concatenate(
        [part.reshape(devices, -1) for part in vector_parts]
        + [jnp.broadcast_to(loss_part, (devices, 1))],
        axis=1,
    )
    vector_sums = jnp.sum(exchange(vector_parts), axis=0)
    *param_sums, small = lax.psum((*param_grads, vector_sums), "dp")
    loss_value = small[-1] / (2.0 * valid_total * D)

    def split_columns(array_in, weight_list):
        results = []
        offset = 0
        for weight in weight_list:
            count = weight.shape[-1]
            piece = array_in[:, offset : offset + count].astype(jnp.float32)
            results.append(piece.reshape(weight.shape))
            offset += count
        return results

    value_g, shared_g = split_columns(value_sum, [w_value, w_shared])
    reset_g, hidden_g, update_g = split_columns(
        rest_sum[:, skip_out:], [w_reset, w_hidden, w_update]
    )
    output_g = jnp.stack(
        [
            rest_sum[:, part * n_out : (part + 1) * n_out].reshape(rows, -1, n_out)
            for part in range(parts_out)
        ],
        axis=1,
    )
    output_g = output_g.astype(jnp.float32).reshape(w_output.shape)
    gate_g, up_g = split_columns(inner_sum, [w_gate, w_up])
    (down_g,) = split_columns(down_sum, [w_down])
    return (
        layer_output,
        loss_value,
        input_grad,
        *param_sums,
        value_g,
        shared_g,
        reset_g,
        hidden_g,
        update_g,
        small[2 * feat_share : 2 * feat_share + z_share],
        small[2 * feat_share + z_share : 2 * feat_share + 2 * z_share],
        small[2 * feat_share + 2 * z_share : 2 * feat_share + 3 * z_share],
        output_g,
        small[:feat_share],
        small[feat_share : 2 * feat_share],
        gate_g,
        up_g,
        down_g,
    )


def solution(mesh):
    in_specs = (
        P(("row", "col"), "dp"),
        P(("row", "col"), "dp"),
        P("dp"),
        P("dp"),
        P(("row", "col")),
        P(("row", "col")),
        P(("row", "col"), None),
        P(("row", "col"), None),
        P(("row", "col"), None),
        P(("row", "col"), None),
        P(("row", "col"), None),
        P(("row", "col")),
        P(None, "col", None, "row"),
        P(None, "col", None, "row"),
        P(None, "col", None, "row"),
        P(None, "col", None, "row"),
        P(None, "col", None, "row"),
        P(("row", "col")),
        P(("row", "col")),
        P(("row", "col")),
        P(None, "col", None, "row"),
        P(("row", "col")),
        P(("row", "col")),
        P(None, "col", None, "row"),
        P(None, "col", None, "row"),
        P(None, "col", None, "row"),
    )
    out_specs = (
        P(("row", "col"), "dp"),
        P(),
        P(("row", "col"), "dp"),
        P(("row", "col")),
        P(("row", "col")),
        P(("row", "col"), None),
        P(("row", "col"), None),
        P(("row", "col"), None),
        P(("row", "col"), None),
        P(("row", "col"), None),
        P(("row", "col")),
        P(None, "col", None, "row"),
        P(None, "col", None, "row"),
        P(None, "col", None, "row"),
        P(None, "col", None, "row"),
        P(None, "col", None, "row"),
        P(("row", "col")),
        P(("row", "col")),
        P(("row", "col")),
        P(None, "col", None, "row"),
        P(("row", "col")),
        P(("row", "col")),
        P(None, "col", None, "row"),
        P(None, "col", None, "row"),
        P(None, "col", None, "row"),
    )
    return jax.shard_map(shards, mesh=mesh, in_specs=in_specs, out_specs=out_specs, check_vma=False)
```

```python
from functools import partial

import jax
import jax.numpy as jnp
from jax import lax
from jax.experimental import pallas as pl
from jax.experimental.pallas import tpu as pltpu
from jax.sharding import PartitionSpec as P

D = 1024
Z = 256
SPAN = 2048
GS = 32
UNIT = 128
STATES = 16
COUNT_ROWS = 256
TILE = 256
BATCH = 16
BATCH_BACK = 16

EPSILON = 1e-05
NEGATIVE = -1000000000.0


def expected(weight):
    return pl.CostEstimate(flops=weight * 1150000000, bytes_accessed=0, transcendentals=0)


NT = (((1,), (1,)), ((), ()))
NN = (((1,), (0,)), ((), ()))
TN = (((0,), (0,)), ((), ()))


def halves(array_in):
    high = array_in.astype(jnp.bfloat16)
    return high, (array_in - high.astype(jnp.float32)).astype(jnp.bfloat16)


def dot_split(left, right, dims):
    left_high, left_low = left
    right_high, right_low = right
    product = partial(lax.dot_general, dimension_numbers=dims, preferred_element_type=jnp.float32)
    return (
        product(left_high, right_high)
        + product(left_low, right_high)
        + product(left_high, right_low)
    )


def dot_exact(left, right):
    return lax.dot_general(
        left, right, NN, precision=lax.Precision.HIGHEST, preferred_element_type=jnp.float32
    )


def toeplitz(kernel_row):
    rows = lax.broadcasted_iota(jnp.int32, (UNIT, UNIT), 0)
    lanes = lax.broadcasted_iota(jnp.int32, (UNIT, UNIT), 1)
    spread = pltpu.roll(
        jnp.broadcast_to(kernel_row, (UNIT, UNIT)), 0, 1, stride=1, stride_axis=0
    )
    return jnp.where(lanes >= rows, spread, 0.0)


def lag_sums(products):
    rows = lax.broadcasted_iota(jnp.int32, (UNIT, UNIT), 0)
    lanes = lax.broadcasted_iota(jnp.int32, (UNIT, UNIT), 1)
    kept = jnp.where(rows + lanes >= UNIT - 1, products, 0.0)
    aligned = pltpu.roll(kept, 0, 1, stride=1, stride_axis=0)
    return pltpu.roll(jnp.sum(aligned, axis=0, keepdims=True), 1, 1)


def reversed_lanes(parts):
    rows = lax.broadcasted_iota(jnp.int32, (UNIT, UNIT), 0)
    lanes = lax.broadcasted_iota(jnp.int32, (UNIT, UNIT), 1)
    mirror = (rows + lanes == UNIT - 1).astype(jnp.bfloat16)
    return tuple(
        lax.dot_general(part, mirror, NN, preferred_element_type=jnp.float32).astype(jnp.bfloat16)
        for part in parts
    )


def power_tables(turn_re, turn_im):
    lanes = lax.broadcasted_iota(jnp.int32, (STATES, UNIT), 1)
    now_re = jnp.broadcast_to(turn_re, (STATES, UNIT))
    now_im = jnp.broadcast_to(turn_im, (STATES, UNIT))
    up_re = jnp.ones((STATES, UNIT), jnp.float32)
    up_im = jnp.zeros((STATES, UNIT), jnp.float32)
    down_re, down_im = up_re, up_im
    for bit in range(UNIT.bit_length() - 1):
        is_set = ((lanes >> bit) & 1) == 1
        next_re = up_re * now_re - up_im * now_im
        next_im = up_re * now_im + up_im * now_re
        fall_re = down_re * now_re - down_im * now_im
        fall_im = down_re * now_im + down_im * now_re
        up_re, up_im = jnp.where(is_set, next_re, up_re), jnp.where(is_set, next_im, up_im)
        down_re = jnp.where(is_set, down_re, fall_re)
        down_im = jnp.where(is_set, down_im, fall_im)
        now_re, now_im = now_re * now_re - now_im * now_im, 2.0 * now_re * now_im
    return up_re, up_im, down_re, down_im, now_re, now_im


def state_scan(ends_re, ends_im, leap_re, leap_im, allowed, units, sign):
    lanes = lax.broadcasted_iota(jnp.int32, ends_re.shape, 1)
    distance = 1
    while distance < units:
        shift = distance if sign > 0 else units - distance
        past_re = pltpu.roll(ends_re, shift, 1)
        past_im = pltpu.roll(ends_im, shift, 1)
        keep = allowed(lanes, distance)
        past_re = jnp.where(keep, past_re, 0.0)
        past_im = jnp.where(keep, past_im, 0.0)
        ends_re, ends_im = (
            ends_re + leap_re * past_re - leap_im * past_im,
            ends_im + leap_re * past_im + leap_im * past_re,
        )
        leap_re, leap_im = leap_re * leap_re - leap_im * leap_im, 2.0 * leap_re * leap_im
        distance *= 2
    shift = 1 if sign > 0 else units - 1
    keep = allowed(lanes, 1)
    return (
        jnp.where(keep, pltpu.roll(ends_re, shift, 1), 0.0),
        jnp.where(keep, pltpu.roll(ends_im, shift, 1), 0.0),
    )


def front_forward_kernel(
    places,
    units,
    start_row,
    start_col,
    x_ref,
    teacher_ref,
    state_ref,
    channel_ref,
    send_ref,
    mixed_ref,
    plain_ref,
    pre_ref,
    stat_ref,
    table_ref,
    row_ref,
    hold_ref,
    normed_ref,
    sums_ref,
    ends_ref,
):
    f32 = jnp.float32
    rows = lax.broadcasted_iota(jnp.int32, (UNIT, UNIT), 0)
    lanes = lax.broadcasted_iota(jnp.int32, (UNIT, UNIT), 1)
    upper = (rows <= lanes).astype(f32)
    for unit in range(units):
        tile = x_ref[:, unit * UNIT : (unit + 1) * UNIT]
        sums_ref[unit : unit + 1, :] = jnp.sum(tile, axis=0, keepdims=True)
        sums_ref[units + unit : units + unit + 1, :] = jnp.sum(tile * tile, axis=0, keepdims=True)
    inside = dot_exact(sums_ref[...], upper)
    starts = start_col[...]
    later = lax.broadcasted_iota(jnp.int32, (units, units), 0)
    sooner = lax.broadcasted_iota(jnp.int32, (units, units), 1)
    before = ((sooner < later) & (sooner >= starts)).astype(f32)
    totals = jnp.broadcast_to(inside[:, UNIT - 1 : UNIT], (2 * units, UNIT))
    sum_one = inside[:units] + dot_exact(before, totals[:units])
    sum_two = inside[units:] + dot_exact(before, totals[units:])
    unit_at = lax.broadcasted_iota(jnp.int32, (units, UNIT), 0)
    lane_at = lax.broadcasted_iota(jnp.int32, (units, UNIT), 1)
    counted = (GS * ((unit_at - starts) * UNIT + lane_at + 1)).astype(f32)
    mean_val = sum_one / counted
    inv_std = lax.rsqrt(sum_two / counted - mean_val * mean_val + EPSILON)
    stat_ref[0, :units, :] = mean_val
    stat_ref[0, units:, :] = inv_std
    gain, bias, skip = channel_ref[:, 0:1], channel_ref[:, 1:2], channel_ref[:, 2:3]
    for unit in range(units):
        tile = x_ref[:, unit * UNIT : (unit + 1) * UNIT]
        mean_row = stat_ref[0, unit : unit + 1, :]
        std_row = stat_ref[0, units + unit : units + unit + 1, :]
        normed_ref[unit * GS : (unit + 1) * GS, :] = (tile - mean_row) * std_row * gain + bias

    def first_pass(step, unused):
        first = step * BATCH
        many = range(BATCH)
        base = pl.multiple_of(first * STATES, BATCH * STATES)
        params = [state_ref[pl.ds(base + one * STATES, STATES), :] for one in many]
        series = [halves(normed_ref[pl.ds(first + one, units, stride=GS), :]) for one in many]
        tables = [power_tables(params[one][:, 0:1], params[one][:, 1:2]) for one in many]
        ends, mixers, matrices, kernel_rows = [], [], [], []
        for one in many:
            turn_re, turn_im = params[one][:, 0:1], params[one][:, 1:2]
            in_coeff, out_re, out_im = (params[one][:, at : at + 1] for at in (2, 3, 4))
            up_re, up_im, down_re, down_im, _, _ = tables[one]
            out_up_re = out_re * up_re - out_im * up_im
            out_up_im = out_re * up_im + out_im * up_re
            kernel_rows.append(jnp.sum(in_coeff * out_up_re, axis=0, keepdims=True))
            mixers.append(
                jnp.concatenate(
                    [
                        turn_re * out_up_re - turn_im * out_up_im,
                        -(turn_re * out_up_im + turn_im * out_up_re),
                    ],
                    axis=0,
                )
            )
            feed = jnp.concatenate([in_coeff * down_re, in_coeff * down_im], axis=0)
            ends.append(dot_split(halves(feed), series[one], NT))
        starts_row = start_row[...]
        held_re, held_im = state_scan(
            jnp.concatenate([part[:STATES] for part in ends], axis=0),
            jnp.concatenate([part[STATES:] for part in ends], axis=0),
            jnp.concatenate([part[4][:, :units] for part in tables], axis=0),
            jnp.concatenate([part[5][:, :units] for part in tables], axis=0),
            lambda lanes, distance: (lanes - distance) >= starts_row,
            units,
            1,
        )
        smoothed = []
        for one in many:
            span = slice(one * STATES, (one + 1) * STATES)
            held = jnp.concatenate([held_re[span], held_im[span]], axis=0)
            smoothed.append(
                dot_split(series[one], halves(toeplitz(kernel_rows[one])), NN)
                + dot_split(halves(held), halves(mixers[one]), TN)
            )
        for index in range(4):
            table_ref[index, pl.ds(base, BATCH * STATES), :] = jnp.concatenate(
                [part[index] for part in tables], axis=0
            )
        hold_ref[0, pl.ds(base, BATCH * STATES), :] = held_re
        hold_ref[1, pl.ds(base, BATCH * STATES), :] = held_im
        for one in many:
            row_ref[pl.ds(first + one, 1), :] = kernel_rows[one]
            ends_ref[pl.ds(first + one, units, stride=GS), :] = smoothed[one]
        return unused

    lax.fori_loop(0, GS // BATCH, first_pass, 0)
    for unit in range(units):
        here = slice(unit * GS, (unit + 1) * GS)
        normed = normed_ref[here, :]
        pre_act = ends_ref[here, :] + skip * normed
        pre_ref[0, here, :] = pre_act
        device, spot = places[unit]
        across = slice(spot * UNIT, (spot + 1) * UNIT)
        span = slice(unit * UNIT, (unit + 1) * UNIT)
        plain_ref[device, 0, :, across] = x_ref[:, span].astype(jnp.bfloat16)
        plain_ref[device, 1, :, across] = teacher_ref[:, span].astype(jnp.bfloat16)
        send_ref[device, :, across] = normed.astype(jnp.bfloat16)
        mixed_ref[device, :, across] = (pre_act * jax.nn.sigmoid(pre_act)).astype(jnp.bfloat16)


def front_backward_kernel(places, units, skipped, *refs):
    (
        start_row,
        stop_row,
        start_col,
        stop_col,
        x_ref,
        state_ref,
        channel_ref,
        normed_grad_ref,
        mixed_grad_ref,
        direct_ref,
        pre_ref,
        stat_ref,
        table_ref,
        row_ref,
        hold_ref,
    ) = refs[:15]
    (
        output_ref,
        out_ref,
        state_grad_ref,
        channel_grad_ref,
        normed_ref,
        slope_ref,
        back_ref,
        sums_ref,
    ) = refs[15 + skipped :]
    f32 = jnp.float32
    gain, bias, skip = channel_ref[:, 0:1], channel_ref[:, 1:2], channel_ref[:, 2:3]
    skip_sum = jnp.zeros((GS, UNIT), f32)
    for unit in range(units):
        here = slice(unit * GS, (unit + 1) * GS)
        device, spot = places[unit]
        across = slice(spot * UNIT, (spot + 1) * UNIT)
        tile = x_ref[:, unit * UNIT : (unit + 1) * UNIT]
        mean_row = stat_ref[0, unit : unit + 1, :]
        std_row = stat_ref[0, units + unit : units + unit + 1, :]
        normed = (tile - mean_row) * std_row * gain + bias
        normed_ref[here, :] = normed
        pre_act = pre_ref[0, here, :]
        logistic = jax.nn.sigmoid(pre_act)
        slope = (
            mixed_grad_ref[device, :, across].astype(f32)
            * logistic
            * (1.0 + pre_act * (1.0 - logistic))
        )
        slope_ref[here, :] = slope
        skip_sum = skip_sum + slope * normed
    channel_grad_ref[:, 2:3] = jnp.sum(skip_sum, axis=1, keepdims=True)

    lag = lax.broadcasted_iota(jnp.int32, (STATES, UNIT), 1).astype(f32)

    def channel_pass(step, unused):
        first = step * BATCH_BACK
        many = range(BATCH_BACK)
        base = pl.multiple_of(first * STATES, BATCH_BACK * STATES)

        def pick(ref_at):
            return [ref_at[one * STATES : (one + 1) * STATES] for one in many]

        rows_here = pl.ds(base, BATCH_BACK * STATES)
        params = pick(state_ref[rows_here, :])
        up_re_all, up_im_all, down_re_all, down_im_all = (
            pick(table_ref[index, rows_here, :]) for index in range(4)
        )
        held_re_all, held_im_all = (pick(hold_ref[index, rows_here, :]) for index in range(2))
        kernel_rows = [row_ref[pl.ds(first + one, 1), :] for one in many]
        slopes = [halves(slope_ref[pl.ds(first + one, units, stride=GS), :]) for one in many]
        series = [halves(normed_ref[pl.ds(first + one, units, stride=GS), :]) for one in many]
        nexts, mixes, pulled = [], [], []
        for one in many:
            turn_re, turn_im = params[one][:, 0:1], params[one][:, 1:2]
            out_re, out_im = params[one][:, 3:4], params[one][:, 4:5]
            next_re = turn_re * up_re_all[one] - turn_im * up_im_all[one]
            next_im = turn_re * up_im_all[one] + turn_im * up_re_all[one]
            mix_re = out_re * next_re - out_im * next_im
            mix_im = out_re * next_im + out_im * next_re
            nexts.append((next_re, next_im))
            mixes.append((mix_re, mix_im))
            pulled.append(
                dot_split(halves(jnp.concatenate([mix_re, -mix_im], axis=0)), slopes[one], NT)
            )
        stops_row = stop_row[...]
        leaps_re = [jnp.broadcast_to(part[:, 5:6], (STATES, units)) for part in params]
        leaps_im = [jnp.broadcast_to(-part[:, 6:7], (STATES, units)) for part in params]
        pull_re_all, pull_im_all = state_scan(
            jnp.concatenate([part[:STATES] for part in pulled], axis=0),
            jnp.concatenate([part[STATES:] for part in pulled], axis=0),
            jnp.concatenate(leaps_re, axis=0),
            jnp.concatenate(leaps_im, axis=0),
            lambda lanes, distance: (lanes + distance) <= stops_row,
            units,
            -1,
        )
        pull_re_all, pull_im_all = pick(pull_re_all), pick(pull_im_all)
        backs, columns = [], []
        for one in many:
            in_coeff, out_re, out_im = (params[one][:, at : at + 1] for at in (2, 3, 4))
            leap_re, leap_im = params[one][:, 5:6], params[one][:, 6:7]
            up_re, up_im = up_re_all[one], up_im_all[one]
            down_re, down_im = down_re_all[one], down_im_all[one]
            (next_re, next_im), (mix_re, mix_im) = nexts[one], mixes[one]
            pull_re, pull_im = pull_re_all[one], pull_im_all[one]
            held_re, held_im = held_re_all[one], held_im_all[one]
            pull = halves(jnp.concatenate([pull_re, pull_im], axis=0))
            held = halves(jnp.concatenate([held_re, held_im], axis=0))
            feed_re, feed_im = in_coeff * down_re, in_coeff * down_im
            feed = halves(jnp.concatenate([feed_re, feed_im], axis=0))
            matrix = halves(toeplitz(kernel_rows[one]))
            backs.append(dot_split(slopes[one], matrix, NT) + dot_split(pull, feed, TN))
            lags = lag_sums(dot_split(slopes[one], reversed_lanes(series[one]), TN))
            mix_grad = dot_split(held, slopes[one], NN)
            feed_grad = dot_split(pull, series[one], NN)
            mg_re, mg_im = mix_grad[:STATES], -mix_grad[STATES:]
            fg_re, fg_im = feed_grad[:STATES], feed_grad[STATES:]
            leap_grad_re = held_re * pull_re + held_im * pull_im
            leap_grad_im = held_re * pull_im - held_im * pull_re
            leap_grad_re = jnp.sum(leap_grad_re, axis=1, keepdims=True)
            leap_grad_im = jnp.sum(leap_grad_im, axis=1, keepdims=True)
            lag_up_re, lag_up_im = lags * up_re, lags * up_im
            out_grad_re = jnp.sum(
                in_coeff * lag_up_re + mg_re * next_re + mg_im * next_im, axis=1, keepdims=True
            )
            out_grad_im = jnp.sum(
                -in_coeff * lag_up_im + mg_im * next_re - mg_re * next_im, axis=1, keepdims=True
            )
            tap_re = out_re * lag_up_re - out_im * lag_up_im
            tap_im = out_re * lag_up_im + out_im * lag_up_re
            in_grad = jnp.sum(tap_re + fg_re * down_re + fg_im * down_im, axis=1, keepdims=True)
            log_re = jnp.sum(
                lag * in_coeff * tap_re
                + (lag + 1.0) * (mix_re * mg_re + mix_im * mg_im)
                + (UNIT - 1.0 - lag) * (feed_re * fg_re + feed_im * fg_im),
                axis=1,
                keepdims=True,
            ) + UNIT * (leap_re * leap_grad_re + leap_im * leap_grad_im)
            log_im = jnp.sum(
                -lag * in_coeff * tap_im
                + (lag + 1.0) * (mix_re * mg_im - mix_im * mg_re)
                + (UNIT - 1.0 - lag) * (feed_re * fg_im - feed_im * fg_re),
                axis=1,
                keepdims=True,
            ) + UNIT * (leap_re * leap_grad_im - leap_im * leap_grad_re)
            columns.append((log_re, log_im, in_grad, out_grad_re, out_grad_im))
        for one in many:
            back_ref[pl.ds(first + one, units, stride=GS), :] = backs[one]
        for index in range(5):
            state_grad_ref[rows_here, index : index + 1] = jnp.concatenate(
                [part[index] for part in columns], axis=0
            )
        return unused

    lax.fori_loop(0, GS // BATCH_BACK, channel_pass, 0)

    gain_sum = jnp.zeros((GS, UNIT), f32)
    bias_sum = jnp.zeros((GS, UNIT), f32)
    for unit in range(units):
        here = slice(unit * GS, (unit + 1) * GS)
        device, spot = places[unit]
        across = slice(spot * UNIT, (spot + 1) * UNIT)
        tile = x_ref[:, unit * UNIT : (unit + 1) * UNIT]
        mean_row = stat_ref[0, unit : unit + 1, :]
        std_row = stat_ref[0, units + unit : units + unit + 1, :]
        plain = (tile - mean_row) * std_row
        total = (
            normed_grad_ref[device, :, across].astype(f32)
            + skip * slope_ref[here, :]
            + back_ref[here, :]
        )
        gain_sum = gain_sum + total * plain
        bias_sum = bias_sum + total
        scaled = total * gain
        back_ref[here, :] = scaled
        sums_ref[unit : unit + 1, :] = jnp.sum(scaled, axis=0, keepdims=True)
        sums_ref[units + unit : units + unit + 1, :] = jnp.sum(
            scaled * plain, axis=0, keepdims=True
        )
    channel_grad_ref[:, 0:1] = jnp.sum(gain_sum, axis=1, keepdims=True)
    channel_grad_ref[:, 1:2] = jnp.sum(bias_sum, axis=1, keepdims=True)
    mean_val, inv_std = stat_ref[0, :units, :], stat_ref[0, units:, :]
    var_grad = -0.5 * inv_std * inv_std * sums_ref[units:, :]
    mean_grad = -inv_std * sums_ref[:units, :] - 2.0 * mean_val * var_grad
    unit_at = lax.broadcasted_iota(jnp.int32, (units, UNIT), 0)
    lane_at = lax.broadcasted_iota(jnp.int32, (units, UNIT), 1)
    counted = (GS * ((unit_at - start_col[...]) * UNIT + lane_at + 1)).astype(f32)
    sums_ref[:units, :] = mean_grad / counted
    sums_ref[units:, :] = var_grad / counted
    rows = lax.broadcasted_iota(jnp.int32, (UNIT, UNIT), 0)
    lanes = lax.broadcasted_iota(jnp.int32, (UNIT, UNIT), 1)
    inside = dot_exact(sums_ref[...], (rows >= lanes).astype(f32))
    sooner = lax.broadcasted_iota(jnp.int32, (units, units), 0)
    later = lax.broadcasted_iota(jnp.int32, (units, units), 1)
    after = ((later > sooner) & (later <= stop_col[...])).astype(f32)
    totals = jnp.broadcast_to(inside[:, 0:1], (2 * units, UNIT))
    sums_ref[:units, :] = inside[:units] + dot_exact(after, totals[:units])
    sums_ref[units:, :] = 2.0 * (inside[units:] + dot_exact(after, totals[units:]))
    for unit in range(units):
        here = slice(unit * GS, (unit + 1) * GS)
        device, spot = places[unit]
        across = slice(spot * UNIT, (spot + 1) * UNIT)
        span = slice(unit * UNIT, (unit + 1) * UNIT)
        out_ref[:, span] = (
            back_ref[here, :] * stat_ref[0, units + unit : units + unit + 1, :]
            + sums_ref[unit : unit + 1, :]
            + x_ref[:, span] * sums_ref[units + unit : units + unit + 1, :]
            + direct_ref[device, 0, :, across].astype(f32)
        )
        output_ref[:, span] = direct_ref[device, 1, :, across].astype(f32)


def sequence_bounds(block_first, blocks, units):
    per_block = units // blocks
    index = jnp.arange(units, dtype=jnp.int32)
    begins = jnp.where(
        (index % per_block == 0) & (jnp.repeat(block_first, per_block) == 1), index, 0
    )
    starts = lax.cummax(begins)
    is_start = (index % per_block == 0) & (jnp.repeat(block_first, per_block) == 1)
    following = jnp.where(is_start, index - 1, units - 1)
    shifted = jnp.concatenate([following[1:], jnp.full((1,), units - 1, jnp.int32)])
    stops = lax.cummin(shifted, reverse=True)
    return starts, stops


def whole(shape):
    return pl.BlockSpec(shape, lambda group: (0,) * len(shape))


def front_forward(layer_input, teacher, state_params, channel_params, bounds, places, devices):
    channels, slots = layer_input.shape
    units = slots // UNIT
    tokens = slots // devices
    groups = channels // GS
    starts, stops = bounds
    f32 = jnp.float32
    return pl.pallas_call(
        partial(front_forward_kernel, places, units),
        grid=(groups,),
        in_specs=[
            whole((1, units)),
            whole((units, 1)),
            pl.BlockSpec((GS, slots), lambda group: (group, 0)),
            pl.BlockSpec((GS, slots), lambda group: (group, 0)),
            pl.BlockSpec((GS * STATES, 8), lambda group: (group, 0)),
            pl.BlockSpec((GS, 8), lambda group: (group, 0)),
        ],
        out_specs=[
            pl.BlockSpec((devices, GS, tokens), lambda group: (0, group, 0)),
            pl.BlockSpec((devices, GS, tokens), lambda group: (0, group, 0)),
            pl.BlockSpec((devices, 2, GS, tokens), lambda group: (0, 0, group, 0)),
            pl.BlockSpec((1, units * GS, UNIT), lambda group: (group, 0, 0)),
            pl.BlockSpec((1, 2 * units, UNIT), lambda group: (group, 0, 0)),
            pl.BlockSpec((4, GS * STATES, UNIT), lambda group: (0, group, 0)),
            pl.BlockSpec((GS, UNIT), lambda group: (group, 0)),
            pl.BlockSpec((2, GS * STATES, units), lambda group: (0, group, 0)),
        ],
        out_shape=[
            jax.ShapeDtypeStruct((devices, channels, tokens), jnp.bfloat16),
            jax.ShapeDtypeStruct((devices, channels, tokens), jnp.bfloat16),
            jax.ShapeDtypeStruct((devices, 2, channels, tokens), jnp.bfloat16),
            jax.ShapeDtypeStruct((groups, units * GS, UNIT), f32),
            jax.ShapeDtypeStruct((groups, 2 * units, UNIT), f32),
            jax.ShapeDtypeStruct((4, channels * STATES, UNIT), f32),
            jax.ShapeDtypeStruct((channels, UNIT), f32),
            jax.ShapeDtypeStruct((2, channels * STATES, units), f32),
        ],
        scratch_shapes=[
            pltpu.VMEM((units * GS, UNIT), f32),
            pltpu.VMEM((2 * units, UNIT), f32),
            pltpu.VMEM((units * GS, UNIT), f32),
        ],
        cost_estimate=expected(35),
        name="front_forward",
    )(starts[None, :], starts[:, None], layer_input, teacher, state_params, channel_params)


def front_backward(
    layer_input,
    state_params,
    channel_params,
    bounds,
    places,
    devices,
    normed_grads,
    mixed_grads,
    direct,
    saved,
    first=0,
    count=1,
    filled=(),
):
    channels, slots = layer_input.shape
    units = slots // UNIT
    tokens = slots // devices
    groups = channels // GS
    starts, stops = bounds
    f32 = jnp.float32
    return pl.pallas_call(
        partial(front_backward_kernel, places, units, len(filled)),
        grid=(count,),
        in_specs=[
            whole((1, units)),
            whole((1, units)),
            whole((units, 1)),
            whole((units, 1)),
            pl.BlockSpec((GS, slots), lambda group: (first + group, 0)),
            pl.BlockSpec((GS * STATES, 8), lambda group: (first + group, 0)),
            pl.BlockSpec((GS, 8), lambda group: (first + group, 0)),
            pl.BlockSpec((devices, GS, tokens), lambda group: (0, first + group, 0)),
            pl.BlockSpec((devices, GS, tokens), lambda group: (0, first + group, 0)),
            pl.BlockSpec((devices, 2, GS, tokens), lambda group: (0, 0, first + group, 0)),
            pl.BlockSpec((1, units * GS, UNIT), lambda group: (first + group, 0, 0)),
            pl.BlockSpec((1, 2 * units, UNIT), lambda group: (first + group, 0, 0)),
            pl.BlockSpec((4, GS * STATES, UNIT), lambda group: (0, first + group, 0)),
            pl.BlockSpec((GS, UNIT), lambda group: (first + group, 0)),
            pl.BlockSpec((2, GS * STATES, units), lambda group: (0, first + group, 0)),
        ]
        + [pl.BlockSpec(memory_space=pl.ANY)] * len(filled),
        out_specs=[
            pl.BlockSpec((GS, slots), lambda group: (first + group, 0)),
            pl.BlockSpec((GS, slots), lambda group: (first + group, 0)),
            pl.BlockSpec((GS * STATES, 8), lambda group: (first + group, 0)),
            pl.BlockSpec((GS, 8), lambda group: (first + group, 0)),
        ],
        out_shape=[
            jax.ShapeDtypeStruct((channels, slots), f32),
            jax.ShapeDtypeStruct((channels, slots), f32),
            jax.ShapeDtypeStruct((channels * STATES, 8), f32),
            jax.ShapeDtypeStruct((channels, 8), f32),
        ],
        scratch_shapes=[
            pltpu.VMEM((units * GS, UNIT), f32),
            pltpu.VMEM((units * GS, UNIT), f32),
            pltpu.VMEM((units * GS, UNIT), f32),
            pltpu.VMEM((2 * units, UNIT), f32),
        ],
        input_output_aliases={15 + index: index for index in range(len(filled))},
        cost_estimate=expected(20 * count),
        name="front_backward",
    )(
        starts[None, :],
        stops[None, :],
        starts[:, None],
        stops[:, None],
        layer_input,
        state_params,
        channel_params,
        normed_grads,
        mixed_grads,
        direct,
        *saved,
        *filled,
    )


def front_parameters(rate, angle, ema_in, out_re, out_im, gain, bias, skip):
    magnitude = 1.0 - rate
    leap = jnp.exp(UNIT * jnp.log(magnitude))
    columns = [
        magnitude * jnp.cos(angle),
        magnitude * jnp.sin(angle),
        jnp.sqrt(2.0 * rate) * ema_in,
        out_re,
        out_im,
        leap * jnp.cos(UNIT * angle),
        leap * jnp.sin(UNIT * angle),
        rate,
    ]
    states = jnp.stack(columns, axis=-1).reshape(-1, 8)
    channels = jnp.stack([gain, bias, skip] + [skip] * 5, axis=-1)
    return states, channels


def front_parameter_grads(state_grads, channel_grads, rate, ema_in):
    shaped = state_grads.reshape(rate.shape + (8,))
    log_re, log_im, in_grad = shaped[..., 0], shaped[..., 1], shaped[..., 2]
    root = jnp.sqrt(2.0 * rate)
    return (
        channel_grads[:, 0],
        channel_grads[:, 1],
        in_grad * ema_in / root - log_re / (1.0 - rate),
        log_im,
        in_grad * root,
        shaped[..., 3],
        shaped[..., 4],
        channel_grads[:, 2],
    )


def unit_places(slots, devices, blocks):
    units = slots // UNIT
    per_block = units // blocks
    group = devices // blocks
    per_device = per_block // group
    places = [None] * units
    for block in range(blocks):
        for member in range(group):
            if per_device % 2 == 0:
                half = per_device // 2
                mirror = 2 * group - 1 - member
                owned = [member * half + step for step in range(half)]
                owned += [mirror * half + step for step in range(half)]
            else:
                owned = [member * per_device + step for step in range(per_device)]
            for spot, unit in enumerate(owned):
                places[block * per_block + unit] = (block * group + member, spot)
    return places


def chunk_sites(group, tokens):
    if tokens % (2 * UNIT) == 0:
        half = tokens // 2
        sites = [(member, 0) for member in range(group)]
        sites += [(2 * group - 1 - chunk, half) for chunk in range(group, 2 * group)]
        return half, sites
    return tokens, [(member, 0) for member in range(group)]


def query_pieces(group, tokens, member):
    half, sites = chunk_sites(group, tokens)
    if half < tokens:
        return half, [(member, 0), (2 * group - 1 - member, half)]
    return half, [(member, 0)]


def masked_scores(turned, keys, allowed, scale):
    products = lax.dot_general(turned, keys, NN, preferred_element_type=jnp.float32) * scale
    return jnp.where(allowed, products, NEGATIVE)


def causal_tile(size, key_chunk, query_chunk):
    rows = lax.broadcasted_iota(jnp.int32, (size, size), 0)
    lanes = lax.broadcasted_iota(jnp.int32, (size, size), 1)
    return (lanes <= rows) | (key_chunk < query_chunk)


def attention_forward_kernel(
    group, member_ref, query_ref, key_ref, value_ref, out_ref, log_ref, score_ref, prob_ref
):
    f32, bf16 = jnp.float32, jnp.bfloat16
    tokens = query_ref.shape[1]
    width = out_ref.shape[0]
    member = member_ref[0]
    half, pieces = query_pieces(group, tokens, member)
    _, sites = chunk_sites(group, tokens)
    scale = Z ** (-0.5)
    for chunk, offset in pieces:
        turned = query_ref[:, offset : offset + half].astype(f32).T.astype(bf16)
        log_ref[offset : offset + half, :] = jnp.full((half, UNIT), NEGATIVE, f32)
        out_ref[:, offset : offset + half] = jnp.zeros((width, half), f32)
        for index, (owner, start) in enumerate(sites):

            @pl.when(index <= chunk)
            def _():
                keys = key_ref[owner, :, start : start + half]
                scores = masked_scores(turned, keys, causal_tile(half, index, chunk), scale)
                score_ref[index] = scores
                log_ref[offset : offset + half, :] = jnp.maximum(
                    log_ref[offset : offset + half, :], jnp.max(scores, axis=1, keepdims=True)
                )

        tops = log_ref[offset : offset + half, 0:1]
        prob_ref[:, 0:1] = jnp.zeros((half, 1), f32)
        for index in range(len(sites)):

            @pl.when(index <= chunk)
            def _():
                exponent = jnp.exp(score_ref[index] - tops)
                score_ref[index] = exponent
                prob_ref[:, 0:1] += jnp.sum(exponent, axis=1, keepdims=True)

        totals = prob_ref[:, 0:1]
        log_ref[offset : offset + half, :] = jnp.broadcast_to(
            tops + jnp.log(totals), (half, UNIT)
        )
        for index, (owner, start) in enumerate(sites):

            @pl.when(index <= chunk)
            def _():
                probs = (score_ref[index] / totals).astype(bf16)
                values = value_ref[owner, :, start : start + half]
                out_ref[:, offset : offset + half] += lax.dot_general(
                    values, probs, NT, preferred_element_type=f32
                )


def attention_backward_kernel(
    group,
    member_ref,
    query_ref,
    key_ref,
    value_ref,
    bend_ref,
    grad_ref,
    log_ref,
    query_grad_ref,
    key_out_ref,
    value_out_ref,
    prob_ref,
    slope_ref,
    low_ref,
    score_grad_ref,
    dot_ref,
    turned_ref,
):
    f32, bf16 = jnp.float32, jnp.bfloat16
    tokens = query_ref.shape[1]
    width = grad_ref.shape[0]
    member = member_ref[0]
    half, pieces = query_pieces(group, tokens, member)
    _, sites = chunk_sites(group, tokens)
    scale = Z ** (-0.5)
    for which, (chunk, offset) in enumerate(pieces):
        here = slice(offset, offset + half)
        turned = query_ref[:, here].astype(f32).T.astype(bf16)
        for start in range(0, width, half):
            turned_ref[:, start : start + half] = (
                grad_ref[start : start + half, here].astype(f32).T.astype(bf16)
            )
        logs = log_ref[here, 0:1]
        dot_ref[...] = jnp.zeros(dot_ref.shape, f32)
        query_grad_ref[:, here] = jnp.zeros((Z, half), f32)
        for index, (owner, start) in enumerate(sites):

            @pl.when(index <= chunk)
            def _():
                keys = key_ref[owner, :, start : start + half]
                scores = masked_scores(turned, keys, causal_tile(half, index, chunk), scale)
                probs = jnp.exp(scores - logs)
                prob_ref[index] = probs
                low_ref[which, index] = probs.astype(bf16)
                slope = lax.dot_general(
                    turned_ref[...],
                    value_ref[owner, :, start : start + half],
                    NN,
                    preferred_element_type=f32,
                )
                slope_ref[index] = slope
                dot_ref[:, 0:1] += jnp.sum(probs * slope, axis=1, keepdims=True)

        dots = dot_ref[:, 0:1]
        for index, (owner, start) in enumerate(sites):

            @pl.when(index <= chunk)
            def _():
                score_grad = (prob_ref[index] * (slope_ref[index] - dots)).astype(bf16)
                score_grad_ref[which, index] = score_grad
                keys = key_ref[owner, :, start : start + half]
                query_grad_ref[:, here] += (
                    lax.dot_general(keys, score_grad, NT, preferred_element_type=f32) * scale
                )

    last = pieces[-1]
    for index, (owner, start) in enumerate(sites):
        there = slice(start, start + half)

        def emit(used):
            value_sum, key_sum = None, None
            for which in used:
                offset = pieces[which][1]
                here = slice(offset, offset + half)
                value_part = lax.dot_general(
                    grad_ref[:, here], low_ref[which, index], NN, preferred_element_type=f32
                )
                key_part = lax.dot_general(
                    query_ref[:, here], score_grad_ref[which, index], NN, preferred_element_type=f32
                )
                value_sum = value_part if value_sum is None else value_sum + value_part
                key_sum = key_part if key_sum is None else key_sum + key_part
            value_out_ref[owner, :, there] = (
                value_sum * bend_ref[owner, :, there].astype(f32)
            ).astype(bf16)
            key_out_ref[owner, :, there] = (key_sum * scale).astype(bf16)

        if len(pieces) == 2:

            @pl.when(index <= pieces[0][0])
            def _():
                emit((0, 1))

            @pl.when((index > pieces[0][0]) & (index <= last[0]))
            def _():
                emit((1,))

        else:

            @pl.when(index <= last[0])
            def _():
                emit((0,))

        @pl.when(index > last[0])
        def _():
            value_out_ref[owner, :, there] = jnp.zeros((width, half), bf16)
            key_out_ref[owner, :, there] = jnp.zeros((Z, half), bf16)


VMEM_BUDGET = 60 * 1024 * 1024


def attention_forward(member, queries, keys, values, group):
    tokens = queries.shape[1]
    width = values.shape[1]
    half, sites = chunk_sites(group, tokens)
    f32 = jnp.float32
    vmem = pl.BlockSpec(memory_space=pltpu.VMEM)
    return pl.pallas_call(
        partial(attention_forward_kernel, group),
        in_specs=[pl.BlockSpec(memory_space=pltpu.SMEM)] + [vmem] * 3,
        out_specs=[vmem, vmem],
        out_shape=[
            jax.ShapeDtypeStruct((width, tokens), f32),
            jax.ShapeDtypeStruct((tokens, UNIT), f32),
        ],
        scratch_shapes=[
            pltpu.VMEM((len(sites), half, half), f32),
            pltpu.VMEM((half, UNIT), f32),
        ],
        compiler_params=pltpu.CompilerParams(vmem_limit_bytes=VMEM_BUDGET),
        cost_estimate=expected(16),
        name="attention_forward",
    )(member, queries, keys, values)


def attention_backward(member, queries, keys, values, bends, grads, logs, group):
    tokens = queries.shape[1]
    half, sites = chunk_sites(group, tokens)
    count = tokens // half
    f32, bf16 = jnp.float32, jnp.bfloat16
    vmem = pl.BlockSpec(memory_space=pltpu.VMEM)
    return pl.pallas_call(
        partial(attention_backward_kernel, group),
        in_specs=[pl.BlockSpec(memory_space=pltpu.SMEM)] + [vmem] * 6,
        out_specs=[vmem] * 3,
        out_shape=[
            jax.ShapeDtypeStruct(queries.shape, f32),
            jax.ShapeDtypeStruct(keys.shape, bf16),
            jax.ShapeDtypeStruct(values.shape, bf16),
        ],
        scratch_shapes=[
            pltpu.VMEM((len(sites), half, half), f32),
            pltpu.VMEM((len(sites), half, half), f32),
            pltpu.VMEM((count, len(sites), half, half), bf16),
            pltpu.VMEM((count, len(sites), half, half), bf16),
            pltpu.VMEM((half, UNIT), f32),
            pltpu.VMEM((half, grads.shape[0]), bf16),
        ],
        compiler_params=pltpu.CompilerParams(vmem_limit_bytes=VMEM_BUDGET),
        cost_estimate=expected(8),
        name="attention_backward",
    )(member, queries, keys, values, bends, grads, logs)


def values_kernel(weight_ref, source_ref, value_ref, slope_ref, turned_ref):
    @pl.when(pl.program_id(1) == 0)
    def _():
        width = weight_ref.shape[2]
        for start in range(0, width, TILE):
            turned_ref[start : start + TILE, :] = (
                weight_ref[0, :, start : start + TILE].astype(jnp.float32).T.astype(jnp.bfloat16)
            )

    product = jnp.dot(turned_ref[...], source_ref[0], preferred_element_type=jnp.float32)
    logistic = jax.nn.sigmoid(product)
    value_ref[0] = (product * logistic).astype(jnp.bfloat16)
    slope_ref[0] = (logistic * (1.0 + product * (1.0 - logistic))).astype(jnp.bfloat16)


def block_values(weights, sources, count):
    rows, depth = weights.shape[:2]
    group, _, tokens = sources.shape
    return pl.pallas_call(
        values_kernel,
        grid=(rows, group),
        in_specs=[
            pl.BlockSpec((1, depth, count), lambda part, step: (part, 0, 0)),
            pl.BlockSpec((1, depth, tokens), lambda part, step: (step, 0, 0)),
        ],
        out_specs=[
            pl.BlockSpec((1, count, tokens), lambda part, step: (step, part, 0)),
            pl.BlockSpec((1, count, tokens), lambda part, step: (step, part, 0)),
        ],
        out_shape=[jax.ShapeDtypeStruct((group, rows * count, tokens), jnp.bfloat16)] * 2,
        scratch_shapes=[pltpu.VMEM((count, depth), jnp.bfloat16)],
        compiler_params=pltpu.CompilerParams(vmem_limit_bytes=VMEM_BUDGET),
        cost_estimate=expected(19),
        name="block_values",
    )(weights, sources)


def values_back_kernel(weight_ref, grad_ref, out_ref):
    count = weight_ref.shape[2]
    total = None
    for part in range(weight_ref.shape[0]):
        piece = jnp.dot(
            weight_ref[part],
            grad_ref[0, part * count : (part + 1) * count, :],
            preferred_element_type=jnp.float32,
        )
        total = piece if total is None else total + piece
    out_ref[0] = total.astype(jnp.bfloat16)


def block_values_back(weights, grads, count):
    rows, depth = weights.shape[:2]
    group, width, tokens = grads.shape
    return pl.pallas_call(
        values_back_kernel,
        grid=(group,),
        in_specs=[
            pl.BlockSpec((rows, depth, count), lambda step: (0, 0, 0)),
            pl.BlockSpec((1, width, tokens), lambda step: (step, 0, 0)),
        ],
        out_specs=pl.BlockSpec((1, depth, tokens), lambda step: (step, 0, 0)),
        out_shape=jax.ShapeDtypeStruct((group, depth, tokens), jnp.bfloat16),
        compiler_params=pltpu.CompilerParams(vmem_limit_bytes=VMEM_BUDGET),
        cost_estimate=expected(5),
        name="block_values_back",
    )(weights, grads)


def values_products_kernel(source_ref, grad_ref, out_ref):
    total = None
    for step in range(source_ref.shape[0]):
        piece = lax.dot_general(
            source_ref[step], grad_ref[step], NT, preferred_element_type=jnp.float32
        )
        total = piece if total is None else total + piece
    out_ref[0] = total.astype(jnp.bfloat16)


def block_values_products(rows, sources, grads):
    group, depth, tokens = sources.shape
    width = grads.shape[1]
    count = width // rows
    return pl.pallas_call(
        values_products_kernel,
        grid=(rows,),
        in_specs=[
            pl.BlockSpec((group, depth, tokens), lambda part: (0, 0, 0)),
            pl.BlockSpec((group, count, tokens), lambda part: (0, part, 0)),
        ],
        out_specs=pl.BlockSpec((1, depth, count), lambda part: (part, 0, 0)),
        out_shape=jax.ShapeDtypeStruct((rows, depth, count), jnp.bfloat16),
        compiler_params=pltpu.CompilerParams(vmem_limit_bytes=VMEM_BUDGET),
        cost_estimate=expected(5),
        name="block_values_products",
    )(sources, grads)


def packed_pieces(rows, deep, columns):
    pieces = []
    start = 0
    while start < rows * deep:
        block, inside = divmod(start, UNIT)
        count = min(UNIT - inside, deep - start % deep)
        if block < 4:
            side, lane = (block // 2) * UNIT + inside, (block % 2) * columns
            pieces.append((start, count, side, lane, columns, 0))
        else:
            for part in range(2):
                pieces.append(
                    (
                        start,
                        count,
                        part * UNIT + inside,
                        2 * columns,
                        columns // 2,
                        part * (columns // 2),
                    )
                )
        start += count
    return pieces


def inner_kernel(
    rows,
    cols,
    arrays,
    first_ref,
    teacher_ref,
    mask_ref,
    factor_ref,
    gain_ref,
    bias_ref,
    *refs,
):
    inner_hbm, down_hbm = refs[0], refs[1] if arrays == 2 else None
    inner_body(
        rows,
        cols,
        first_ref,
        teacher_ref,
        mask_ref,
        factor_ref,
        gain_ref,
        bias_ref,
        inner_hbm,
        down_hbm,
        *refs[arrays:],
    )


def inner_body(
    rows,
    cols,
    first_ref,
    teacher_ref,
    mask_ref,
    factor_ref,
    gain_ref,
    bias_ref,
    inner_hbm,
    down_hbm,
    out_ref,
    loss_ref,
    norm_ref,
    act_ref,
    low_ref,
    grads_ref,
    first_grad_ref,
    gain_sum_ref,
    bias_sum_ref,
    inner_ref,
    down_ref,
    turned_ref,
    gate_ref,
    up_ref,
    act_turned_ref,
    inner_sem,
    down_sem,
):
    f32, bf16 = jnp.float32, jnp.bfloat16
    width = first_ref.shape[0]
    tokens = first_ref.shape[1]
    hidden = act_ref.shape[0]
    n_inner = hidden // rows
    n_down = width // rows
    deep = width // (rows * cols)
    deep_down = hidden // (rows * cols)

    packed = down_hbm is None

    def inner_copies():
        copies = []
        for row in range(rows):
            for col in range(cols):
                target = inner_ref.at[:, pl.ds((row * cols + col) * deep, deep)]
                if packed:
                    source = inner_hbm.at[:, col, pl.ds(row * deep, deep), pl.ds(0, 2 * n_inner)]
                else:
                    source = inner_hbm.at[:, col, row]
                copies.append(
                    pltpu.make_async_copy(source, target, inner_sem.at[row * cols + col])
                )
        return copies

    def down_copies():
        copies = []
        for col in range(cols):
            if packed:
                for start, count, side, lane, width_, column in packed_pieces(
                    rows, deep_down, n_down
                ):
                    row, inside = start // deep_down, start % deep_down
                    source = inner_hbm.at[
                        :, col, pl.ds(side, count), pl.ds(2 * n_inner + lane, width_)
                    ]
                    target = down_ref.at[
                        :,
                        pl.ds((row * cols + col) * deep_down + inside, count),
                        pl.ds(column, width_),
                    ]
                    copies.append(pltpu.make_async_copy(source, target, down_sem.at[len(copies)]))
            else:
                for row in range(rows):
                    target = down_ref.at[:, pl.ds((row * cols + col) * deep_down, deep_down)]
                    copies.append(
                        pltpu.make_async_copy(
                            down_hbm.at[:, col, row], target, down_sem.at[len(copies)]
                        )
                    )
        return copies

    for copy in inner_copies():
        copy.start()
    for copy in down_copies():
        copy.start()
    chunk = min(TILE, n_down)
    chunks = [slice(start, start + chunk) for start in range(0, width, chunk)]
    total = jnp.zeros((1, tokens), f32)
    squares = jnp.zeros((1, tokens), f32)
    for here in chunks:
        part = first_ref[here, :]
        total = total + jnp.sum(part, axis=0, keepdims=True)
        squares = squares + jnp.sum(part * part, axis=0, keepdims=True)
    mean_val = total / width
    inv_std = lax.rsqrt(squares / width - mean_val * mean_val + EPSILON)
    for here in chunks:
        unit = (first_ref[here, :] - mean_val) * inv_std
        scaled = unit * gain_ref[here, :] + bias_ref[here, :]
        norm_ref[here, :] = scaled.astype(bf16)
        turned_ref[:, here] = scaled.T.astype(bf16)
    for copy in inner_copies():
        copy.wait()
    tile = min(TILE, n_inner)
    spans = [
        (part, start, min(tile, n_inner - start))
        for part in range(rows)
        for start in range(0, n_inner, tile)
    ]
    for part, start, size in spans:
        gate = jnp.dot(
            turned_ref[...], inner_ref[part, :, start : start + size], preferred_element_type=f32
        )
        up = jnp.dot(
            turned_ref[...],
            inner_ref[part, :, n_inner + start : n_inner + start + size],
            preferred_element_type=f32,
        )
        there = slice(part * n_inner + start, part * n_inner + start + size)
        gate_ref[:, there] = gate
        up_ref[:, there] = up
        act = gate * jax.nn.sigmoid(gate) * up
        act_turned_ref[:, there] = act.astype(bf16)
        act_ref[there, :] = act.T.astype(bf16)
    for copy in down_copies():
        copy.wait()
    factor = factor_ref[0]
    mask = mask_ref[...]
    loss = jnp.zeros((1, tokens), f32)
    for part in range(rows):
        for start in range(0, n_down, chunk):
            delta = jnp.dot(
                act_turned_ref[...],
                down_ref[part, :, start : start + chunk],
                preferred_element_type=f32,
            )
            here = slice(part * n_down + start, part * n_down + start + chunk)
            result = first_ref[here, :] + delta.T
            out_ref[here, :] = result.astype(bf16)
            error = (result - teacher_ref[here, :].astype(f32)) * mask
            loss = loss + jnp.sum(error * error, axis=0, keepdims=True)
            error = error * factor
            first_grad_ref[here, :] = error
            low_ref[part, :, start : start + chunk] = error.T.astype(bf16)
    loss_ref[...] = loss
    for part, start, size in spans:
        there = slice(part * n_inner + start, part * n_inner + start + size)
        back = None
        for other in range(rows):
            piece = lax.dot_general(
                low_ref[other], down_ref[other, there, :], NT, preferred_element_type=f32
            )
            back = piece if back is None else back + piece
        gate, up = gate_ref[:, there], up_ref[:, there]
        logistic = jax.nn.sigmoid(gate)
        grads_ref[part, :, start : start + size] = (
            back * up * logistic * (1.0 + gate * (1.0 - logistic))
        ).astype(bf16)
        grads_ref[part, :, n_inner + start : n_inner + start + size] = (
            back * gate * logistic
        ).astype(bf16)
    mean_one = jnp.zeros((1, tokens), f32)
    mean_two = jnp.zeros((1, tokens), f32)
    for here in chunks:
        back = None
        for part in range(rows):
            piece = lax.dot_general(
                grads_ref[part], inner_ref[part, here, :], NT, preferred_element_type=f32
            )
            back = piece if back is None else back + piece
        back = back.T
        unit = (first_ref[here, :] - mean_val) * inv_std
        gain_sum_ref[here, :] = jnp.sum(back * unit, axis=1, keepdims=True)
        bias_sum_ref[here, :] = jnp.sum(back, axis=1, keepdims=True)
        scaled = back * gain_ref[here, :]
        mean_one = mean_one + jnp.sum(scaled, axis=0, keepdims=True)
        mean_two = mean_two + jnp.sum(scaled * unit, axis=0, keepdims=True)
        first_grad_ref[here, :] = first_grad_ref[here, :] + inv_std * scaled
    mean_one = mean_one / width
    mean_two = mean_two / width
    for here in chunks:
        unit = (first_ref[here, :] - mean_val) * inv_std
        first_grad_ref[here, :] = first_grad_ref[here, :] - inv_std * (
            mean_one + unit * mean_two
        )


def inner_layer(
    rows, cols, first_out, teacher, mask, factor, gain, bias, weights, inner_cols, hidden
):
    width, tokens = first_out.shape
    f32, bf16 = jnp.float32, jnp.bfloat16
    vmem = pl.BlockSpec(memory_space=pltpu.VMEM)
    anywhere = pl.BlockSpec(memory_space=pl.ANY)
    places = rows * cols
    if len(weights) == 1:
        shaped = [weights[0].reshape(rows, cols, -1, weights[0].shape[-1])]
        down_count = cols * len(packed_pieces(rows, hidden // places, width // rows))
    else:
        shaped = [weight.reshape(rows, cols, rows, -1, weight.shape[-1]) for weight in weights]
        down_count = places
    return pl.pallas_call(
        partial(inner_kernel, rows, cols, len(shaped)),
        in_specs=[vmem, vmem, vmem, pl.BlockSpec(memory_space=pltpu.SMEM)]
        + [vmem] * 2
        + [anywhere] * len(shaped),
        out_specs=[vmem] * 9,
        out_shape=[
            jax.ShapeDtypeStruct((width, tokens), bf16),
            jax.ShapeDtypeStruct((1, tokens), f32),
            jax.ShapeDtypeStruct((width, tokens), bf16),
            jax.ShapeDtypeStruct((hidden, tokens), bf16),
            jax.ShapeDtypeStruct((rows, tokens, width // rows), bf16),
            jax.ShapeDtypeStruct((rows, tokens, inner_cols), bf16),
            jax.ShapeDtypeStruct((width, tokens), f32),
            jax.ShapeDtypeStruct((width, 1), f32),
            jax.ShapeDtypeStruct((width, 1), f32),
        ],
        scratch_shapes=[
            pltpu.VMEM((rows, width, inner_cols), bf16),
            pltpu.VMEM((rows, hidden, width // rows), bf16),
            pltpu.VMEM((tokens, width), bf16),
            pltpu.VMEM((tokens, hidden), f32),
            pltpu.VMEM((tokens, hidden), f32),
            pltpu.VMEM((tokens, hidden), bf16),
            pltpu.SemaphoreType.DMA((places,)),
            pltpu.SemaphoreType.DMA((down_count,)),
        ],
        compiler_params=pltpu.CompilerParams(vmem_limit_bytes=VMEM_BUDGET),
        cost_estimate=expected(29),
        name="inner_layer",
    )(first_out, teacher, mask, factor, gain, bias, *shaped)


def packed_products_kernel(inner_ref, inner_grad_ref, down_ref, down_grad_ref, out_ref, hold_ref):
    f32, bf16 = jnp.float32, jnp.bfloat16
    rows, _, depth, _ = inner_ref.shape
    deep = down_ref.shape[2]
    start_at = inner_grad_ref.shape[2]
    columns = down_grad_ref.shape[2]
    for row in range(rows):
        out_ref[0, 0, row * depth : (row + 1) * depth, :start_at] = jnp.dot(
            inner_ref[row, 0], inner_grad_ref[0], preferred_element_type=f32
        ).astype(bf16)
        hold_ref[row * deep : (row + 1) * deep, :] = jnp.dot(
            down_ref[row, 0], down_grad_ref[0], preferred_element_type=f32
        ).astype(bf16)
    for start, count, side, lane, width, column in packed_pieces(rows, deep, columns):
        out_ref[0, 0, side : side + count, start_at + lane : start_at + lane + width] = hold_ref[
            start : start + count, column : column + width
        ]


def packed_products(rows, cols, inner, inner_grads, down, down_grads):
    tokens = inner.shape[1]
    places = rows * cols
    depth, deep = inner.shape[0] // places, down.shape[0] // places
    inner_cols, columns = inner_grads.shape[-1], down_grads.shape[-1]
    total = inner_cols + rows * deep * columns // (rows * depth)
    return pl.pallas_call(
        packed_products_kernel,
        grid=(rows, cols),
        in_specs=[
            pl.BlockSpec((rows, 1, depth, tokens), lambda part, col: (0, col, 0, 0)),
            pl.BlockSpec((1, tokens, inner_cols), lambda part, col: (part, 0, 0)),
            pl.BlockSpec((rows, 1, deep, tokens), lambda part, col: (0, col, 0, 0)),
            pl.BlockSpec((1, tokens, columns), lambda part, col: (part, 0, 0)),
        ],
        out_specs=pl.BlockSpec((1, 1, rows * depth, total), lambda part, col: (part, col, 0, 0)),
        out_shape=jax.ShapeDtypeStruct((rows, cols, rows * depth, total), jnp.bfloat16),
        scratch_shapes=[pltpu.VMEM((rows * deep, columns), jnp.bfloat16)],
        compiler_params=pltpu.CompilerParams(vmem_limit_bytes=VMEM_BUDGET),
        cost_estimate=expected(20),
        name="packed_products",
    )(
        inner.reshape(rows, cols, depth, tokens),
        inner_grads,
        down.reshape(rows, cols, deep, tokens),
        down_grads,
    )


def products_kernel(source_ref, grad_ref, out_ref):
    depth = source_ref.shape[2]
    for row in range(source_ref.shape[0]):
        out_ref[0, 0, row * depth : (row + 1) * depth, :] = jnp.dot(
            source_ref[row, 0], grad_ref[0], preferred_element_type=jnp.float32
        ).astype(jnp.bfloat16)


def local_products(rows, cols, source, grads):
    height, tokens = source.shape
    depth = height // (rows * cols)
    columns = grads.shape[-1]
    return pl.pallas_call(
        products_kernel,
        grid=(rows, cols),
        in_specs=[
            pl.BlockSpec((rows, 1, depth, tokens), lambda part, col: (0, col, 0, 0)),
            pl.BlockSpec((1, tokens, columns), lambda part, col: (part, 0, 0)),
        ],
        out_specs=pl.BlockSpec((1, 1, rows * depth, columns), lambda part, col: (part, col, 0, 0)),
        out_shape=jax.ShapeDtypeStruct((rows, cols, rows * depth, columns), jnp.bfloat16),
        compiler_params=pltpu.CompilerParams(vmem_limit_bytes=VMEM_BUDGET),
        cost_estimate=expected(9 if columns < height else 13),
        name="local_products",
    )(source.reshape(rows, cols, depth, tokens), grads)


PIECES = 2
GATHER_PIECES = 2


def meet_neighbours(side, across):
    barrier = pltpu.get_barrier_semaphore()
    for target in (side, across):
        pl.semaphore_signal(
            barrier, inc=1, device_id={"col": target}, device_id_type=pl.DeviceIdType.MESH
        )
    pl.semaphore_wait(barrier, 2)


def neighbours():
    me = lax.axis_index("col")
    return me, me + 1 - 2 * (me % 2), (me + 2) % 4


def push(source, target, send_sem, recv_sem, device):
    return pltpu.make_async_remote_copy(
        src_ref=source,
        dst_ref=target,
        send_sem=send_sem,
        recv_sem=recv_sem,
        device_id={"col": device},
        device_id_type=pl.DeviceIdType.MESH,
    )


def gather_kernel(
    own_ref, out_ref, local_sem, cross_send, cross_recv, side_send, side_recv, pass_send, pass_recv
):
    me, side, across = neighbours()
    count = own_ref.shape[0] // GATHER_PIECES
    meet_neighbours(side, across)
    crossing = []
    for piece in range(GATHER_PIECES):
        rows = pl.ds(piece * count, count)
        copy = push(
            own_ref.at[rows],
            out_ref.at[me, rows],
            cross_send.at[piece],
            cross_recv.at[piece],
            across,
        )
        copy.start()
        crossing.append(copy)
    beside = push(own_ref, out_ref.at[me], side_send, side_recv, side)
    beside.start()
    local = pltpu.make_async_copy(own_ref, out_ref.at[me], local_sem)
    local.start()
    passing = []
    for piece in range(GATHER_PIECES):
        rows = pl.ds(piece * count, count)
        crossing[piece].wait_recv()
        copy = push(
            out_ref.at[across, rows],
            out_ref.at[across, rows],
            pass_send.at[piece],
            pass_recv.at[piece],
            side,
        )
        copy.start()
        passing.append(copy)
    for piece in range(GATHER_PIECES):
        crossing[piece].wait_send()
        passing[piece].wait()
    beside.wait()
    local.wait()


def gather_members(own):
    dma = pltpu.SemaphoreType.DMA
    anywhere = pl.BlockSpec(memory_space=pl.ANY)
    return pl.pallas_call(
        gather_kernel,
        in_specs=[anywhere],
        out_specs=anywhere,
        out_shape=jax.ShapeDtypeStruct((4,) + own.shape, own.dtype),
        scratch_shapes=[
            dma,
            dma((GATHER_PIECES,)),
            dma((GATHER_PIECES,)),
            dma,
            dma,
            dma((GATHER_PIECES,)),
            dma((GATHER_PIECES,)),
        ],
        compiler_params=pltpu.CompilerParams(collective_id=0, has_side_effects=True),
        cost_estimate=expected(16),
        name="gather_members",
    )(own)


def reduce_kernel(
    parts_ref,
    out_ref,
    beside_ref,
    sum_ref,
    landed_ref,
    first_send,
    first_recv,
    second_send,
    second_recv,
    cross_send,
    cross_recv,
):
    f32, bf16 = jnp.float32, jnp.bfloat16
    me, side, across = neighbours()
    count = out_ref.shape[0] // PIECES
    beyond = (side + 2) % 4
    meet_neighbours(side, across)
    first, second, crossing = [], [], []
    for piece in range(PIECES):
        rows = pl.ds(piece * count, count)
        copy = push(
            parts_ref.at[beyond, rows],
            beside_ref.at[0, rows],
            first_send.at[piece],
            first_recv.at[piece],
            side,
        )
        copy.start()
        first.append(copy)
    for piece in range(PIECES):
        rows = pl.ds(piece * count, count)
        copy = push(
            parts_ref.at[side, rows],
            beside_ref.at[1, rows],
            second_send.at[piece],
            second_recv.at[piece],
            side,
        )
        copy.start()
        second.append(copy)
    for piece in range(PIECES):
        rows = pl.ds(piece * count, count)
        first[piece].wait_recv()
        total = parts_ref[across, rows, :].astype(f32) + beside_ref[0, rows, :].astype(f32)
        sum_ref[rows, :] = total.astype(bf16)
        copy = push(
            sum_ref.at[rows],
            landed_ref.at[rows],
            cross_send.at[piece],
            cross_recv.at[piece],
            across,
        )
        copy.start()
        crossing.append(copy)
    for piece in range(PIECES):
        rows = pl.ds(piece * count, count)
        second[piece].wait_recv()
        crossing[piece].wait_recv()
        out_ref[rows, :] = (
            parts_ref[me, rows, :].astype(f32)
            + beside_ref[1, rows, :].astype(f32)
            + landed_ref[rows, :].astype(f32)
        )
    for piece in range(PIECES):
        first[piece].wait_send()
        second[piece].wait_send()
        crossing[piece].wait_send()


def reduce_members(parts):
    dma = pltpu.SemaphoreType.DMA
    vmem = pl.BlockSpec(memory_space=pltpu.VMEM)
    shape = parts.shape[1:]
    return pl.pallas_call(
        reduce_kernel,
        in_specs=[vmem],
        out_specs=vmem,
        out_shape=jax.ShapeDtypeStruct(shape, jnp.float32),
        scratch_shapes=[
            pltpu.VMEM((2,) + shape, parts.dtype),
            pltpu.VMEM(shape, parts.dtype),
            pltpu.VMEM(shape, parts.dtype),
        ]
        + [dma((PIECES,))] * 6,
        compiler_params=pltpu.CompilerParams(
            collective_id=1, has_side_effects=True, vmem_limit_bytes=VMEM_BUDGET
        ),
        cost_estimate=expected(3),
        name="reduce_members",
    )(parts)


def spread_kernel(
    blocks,
    normed_ref,
    mixed_ref,
    block_ref,
    own_ref,
    local_sem,
    direct_send,
    direct_recv,
    pass_send,
    pass_recv,
    mixed_send,
    mixed_recv,
):
    row, col = lax.axis_index("row"), lax.axis_index("col")
    core, chip = col % 2, col // 2
    group = block_ref.shape[0]
    depth = mixed_ref.shape[1]
    mesh_id = pl.DeviceIdType.MESH

    def spot(of_row, of_col):
        return pl.ds(pl.multiple_of((of_col * blocks + of_row) * depth, depth), depth)

    def other(across, beyond, twin):
        to_row = (row + across) % 2
        to_col = ((chip + beyond) % 2) * 2 + (core + twin) % 2
        return to_row, to_col

    offsets = [(a, b, t) for a in range(2) for b in range(2) for t in range(2)][1:]
    barrier = pltpu.get_barrier_semaphore()
    for offset in offsets:
        to_row, to_col = other(*offset)
        pl.semaphore_signal(
            barrier, inc=1, device_id={"row": to_row, "col": to_col}, device_id_type=mesh_id
        )
    pl.semaphore_wait(barrier, len(offsets))

    mine = spot(row, col)
    direct = []
    for index, offset in enumerate([(0, 1, 0), (1, 0, 0), (1, 1, 0)]):
        to_row, to_col = other(*offset)
        copy = pltpu.make_async_remote_copy(
            src_ref=normed_ref.at[pl.ds(to_row * group, group)],
            dst_ref=block_ref.at[:, mine],
            send_sem=direct_send.at[index],
            recv_sem=direct_recv.at[index],
            device_id={"row": to_row, "col": to_col},
            device_id_type=mesh_id,
        )
        copy.start()
        direct.append(copy)
    side = {"row": row, "col": chip * 2 + (core + 1) % 2}
    passing = []
    own_block = normed_ref.at[pl.ds(row * group, group)]
    copy = pltpu.make_async_remote_copy(
        src_ref=own_block,
        dst_ref=block_ref.at[:, mine],
        send_sem=pass_send.at[3],
        recv_sem=pass_recv.at[3],
        device_id=side,
        device_id_type=mesh_id,
    )
    copy.start()
    passing.append(copy)
    spread = []
    for index, offset in enumerate(offsets):
        to_row, to_col = other(*offset)
        copy = pltpu.make_async_remote_copy(
            src_ref=mixed_ref.at[to_row * 4 + to_col],
            dst_ref=own_ref.at[mine],
            send_sem=mixed_send.at[index],
            recv_sem=mixed_recv.at[index],
            device_id={"row": to_row, "col": to_col},
            device_id_type=mesh_id,
        )
        copy.start()
        spread.append(copy)
    locals_ = [
        pltpu.make_async_copy(own_block, block_ref.at[:, mine], local_sem.at[0]),
        pltpu.make_async_copy(mixed_ref.at[row * 4 + col], own_ref.at[mine], local_sem.at[1]),
    ]
    for copy in locals_:
        copy.start()
    for index, offset in enumerate([(0, 1, 0), (1, 0, 0), (1, 1, 0)]):
        from_row, from_col = other(*offset)
        there = spot(from_row, from_col)
        direct[index].wait_recv()
        copy = pltpu.make_async_remote_copy(
            src_ref=block_ref.at[:, there],
            dst_ref=block_ref.at[:, there],
            send_sem=pass_send.at[index],
            recv_sem=pass_recv.at[index],
            device_id=side,
            device_id_type=mesh_id,
        )
        copy.start()
        passing.append(copy)
    for copy in locals_:
        copy.wait()
    for copy in passing + spread:
        copy.wait()
    for copy in direct:
        copy.wait_send()


def spread_sources(normed, mixed, group):
    dma = pltpu.SemaphoreType.DMA
    anywhere = pl.BlockSpec(memory_space=pl.ANY)
    devices, depth, tokens = normed.shape
    return pl.pallas_call(
        partial(spread_kernel, devices // group),
        in_specs=[anywhere] * 2,
        out_specs=[anywhere] * 2,
        out_shape=[
            jax.ShapeDtypeStruct((group, devices * depth, tokens), normed.dtype),
            jax.ShapeDtypeStruct((devices * depth, tokens), mixed.dtype),
        ],
        scratch_shapes=[
            dma((2,)),
            dma((3,)),
            dma((3,)),
            dma((4,)),
            dma((4,)),
            dma((7,)),
            dma((7,)),
        ],
        compiler_params=pltpu.CompilerParams(collective_id=2, has_side_effects=True),
        cost_estimate=expected(53),
        name="spread_sources",
    )(normed, mixed)


def collect_kernel(
    blocks,
    normed_ref,
    mixed_ref,
    total_ref,
    own_ref,
    beside_ref,
    pair_ref,
    landed_ref,
    local_sem,
    side_send,
    side_recv,
    direct_send,
    direct_recv,
    mixed_send,
    mixed_recv,
):
    f32, bf16 = jnp.float32, jnp.bfloat16
    row, col = lax.axis_index("row"), lax.axis_index("col")
    core, chip = col % 2, col // 2
    group = normed_ref.shape[0]
    depth = own_ref.shape[1]
    mesh_id = pl.DeviceIdType.MESH

    def spot(of_row, of_col):
        return pl.ds(pl.multiple_of((of_col * blocks + of_row) * depth, depth), depth)

    def other(across, beyond, twin):
        to_row = (row + across) % 2
        to_col = ((chip + beyond) % 2) * 2 + (core + twin) % 2
        return to_row, to_col

    offsets = [(a, b, t) for a in range(2) for b in range(2) for t in range(2)][1:]
    chips = [(0, 1), (1, 0), (1, 1), (0, 0)]
    barrier = pltpu.get_barrier_semaphore()
    for offset in offsets:
        to_row, to_col = other(*offset)
        pl.semaphore_signal(
            barrier, inc=1, device_id={"row": to_row, "col": to_col}, device_id_type=mesh_id
        )
    pl.semaphore_wait(barrier, len(offsets))

    side = {"row": row, "col": chip * 2 + (core + 1) % 2}
    beside, direct, spread = [], [], []
    for index, (across, beyond) in enumerate(chips):
        copy = pltpu.make_async_remote_copy(
            src_ref=normed_ref.at[:, spot(*other(across, beyond, 1))],
            dst_ref=beside_ref.at[index],
            send_sem=side_send.at[index],
            recv_sem=side_recv.at[index],
            device_id=side,
            device_id_type=mesh_id,
        )
        copy.start()
        beside.append(copy)
    for index, offset in enumerate(offsets):
        to_row, to_col = other(*offset)
        copy = pltpu.make_async_remote_copy(
            src_ref=mixed_ref.at[spot(to_row, to_col)],
            dst_ref=own_ref.at[row * 4 + col],
            send_sem=mixed_send.at[index],
            recv_sem=mixed_recv.at[index],
            device_id={"row": to_row, "col": to_col},
            device_id_type=mesh_id,
        )
        copy.start()
        spread.append(copy)
    local = pltpu.make_async_copy(
        mixed_ref.at[spot(row, col)], own_ref.at[row * 4 + col], local_sem
    )
    local.start()
    for index, (across, beyond) in enumerate(chips):
        to_row, to_col = other(across, beyond, 0)
        here = spot(to_row, to_col)
        beside[index].wait_recv()
        for step in range(group):
            total = normed_ref[step, here, :].astype(f32) + beside_ref[index, step].astype(f32)
            pair_ref[index, step] = total.astype(bf16)
        if index < 3:
            copy = pltpu.make_async_remote_copy(
                src_ref=pair_ref.at[index],
                dst_ref=landed_ref.at[index],
                send_sem=direct_send.at[index],
                recv_sem=direct_recv.at[index],
                device_id={"row": to_row, "col": to_col},
                device_id_type=mesh_id,
            )
            copy.start()
            direct.append(copy)
    direct[0].wait_recv()
    near = pl.multiple_of(row * group, group)
    far = pl.multiple_of(((row + 1) % 2) * group, group)
    for step in range(group):
        total_ref[near + step] = (
            pair_ref[3, step].astype(f32) + landed_ref[0, step].astype(f32)
        ).astype(bf16)
    direct[1].wait_recv()
    direct[2].wait_recv()
    for step in range(group):
        total_ref[far + step] = (
            landed_ref[1, step].astype(f32) + landed_ref[2, step].astype(f32)
        ).astype(bf16)
    local.wait()
    for copy in spread:
        copy.wait()
    for copy in beside + direct:
        copy.wait_send()


def collect_grads(normed, mixed, devices):
    dma = pltpu.SemaphoreType.DMA
    vmem = pl.BlockSpec(memory_space=pltpu.VMEM)
    anywhere = pl.BlockSpec(memory_space=pl.ANY)
    group, width, tokens = normed.shape
    depth = width // devices
    shape = jax.ShapeDtypeStruct((devices, depth, tokens), normed.dtype)
    return pl.pallas_call(
        partial(collect_kernel, devices // group),
        in_specs=[vmem, anywhere],
        out_specs=[vmem, anywhere],
        out_shape=[shape, shape],
        scratch_shapes=[
            pltpu.VMEM((4, group, depth, tokens), normed.dtype),
            pltpu.VMEM((4, group, depth, tokens), normed.dtype),
            pltpu.VMEM((3, group, depth, tokens), normed.dtype),
            dma,
            dma((4,)),
            dma((4,)),
            dma((3,)),
            dma((3,)),
            dma((7,)),
            dma((7,)),
        ],
        compiler_params=pltpu.CompilerParams(
            collective_id=3, has_side_effects=True, vmem_limit_bytes=VMEM_BUDGET
        ),
        cost_estimate=expected(8),
        name="collect_grads",
    )(normed, mixed)


def silu_slope(pre_act):
    logistic = jax.nn.sigmoid(pre_act)
    return logistic * (1.0 + pre_act * (1.0 - logistic))


def contract_first(left_in, right_in):
    return lax.dot_general(
        left_in, right_in, (((0,), (0,)), ((), ())), preferred_element_type=jnp.float32
    )


def contract_last(left_in, right_in):
    return lax.dot_general(
        left_in, right_in, (((1,), (1,)), ((), ())), preferred_element_type=jnp.float32
    )


def silu(pre_act):
    return pre_act * jax.nn.sigmoid(pre_act)


def swap_blocks(array_in, outer, inner):
    shaped = array_in.reshape(outer, inner, -1, array_in.shape[-1])
    return shaped.transpose(1, 0, 2, 3).reshape(array_in.shape)


def project(weights, source):
    return jnp.concatenate(
        [contract_first(weights[part], source) for part in range(weights.shape[0])], axis=0
    )


def project_back(weights, grads):
    parts = weights.shape[0]
    pieces = grads.reshape(parts, -1, grads.shape[-1])
    total = None
    for part in range(parts):
        product = jnp.dot(weights[part], pieces[part], preferred_element_type=jnp.float32)
        total = product if total is None else total + product
    return total


def weight_products(source, grads, parts):
    pieces = grads.reshape(parts, -1, grads.shape[-1])
    return [contract_last(source, pieces[part]).astype(jnp.bfloat16) for part in range(parts)]


def shards(
    layer_input,
    teacher,
    block_len,
    block_first,
    norm_gain,
    norm_bias,
    ema_rate,
    ema_angle,
    ema_input,
    ema_out_real,
    ema_out_imag,
    ema_skip,
    w_value,
    w_shared,
    w_reset,
    w_hidden,
    w_update,
    query_gain,
    query_bias,
    key_gain,
    w_output,
    final_gain,
    final_bias,
    w_gate,
    w_up,
    w_down,
):
    bf16 = jnp.bfloat16
    grid = ("row", "col")
    rows, cols, dps = lax.axis_size("row"), lax.axis_size("col"), lax.axis_size("dp")
    devices = rows * cols
    slot_count = layer_input.shape[1]
    blocks_here = slot_count // SPAN
    group = devices // blocks_here
    tokens = slot_count // devices
    place = lax.axis_index("row") * cols + lax.axis_index("col")
    my_block = place // group
    member = place % group
    places = unit_places(slot_count, devices, blocks_here)
    state_params, channel_params = front_parameters(
        ema_rate,
        ema_angle,
        ema_input,
        ema_out_real,
        ema_out_imag,
        norm_gain,
        norm_bias,
        ema_skip,
    )
    bounds = sequence_bounds(block_first, blocks_here, slot_count // UNIT)

    def exchange(array_in):
        return lax.all_to_all(array_in, grid, 0, 0, tiled=True)

    def gather_weights(local):
        gathered = lax.all_gather(local, grid, axis=0)
        return gathered.reshape(rows, -1, local.shape[-1])

    def local_matrix(weight_list):
        flat = [weight.reshape(-1, weight.shape[-1]) for weight in weight_list]
        return flat[0] if len(flat) == 1 else jnp.concatenate(flat, axis=1)

    barrier = lax.optimization_barrier
    vectors = exchange(
        jnp.broadcast_to(
            jnp.concatenate([final_gain, final_bias, query_gain, query_bias, key_gain])[None],
            (devices, 2 * final_gain.shape[0] + 3 * query_gain.shape[0]),
        )
    )
    valid_here = jnp.sum(block_len).astype(jnp.float32)
    valid_all = lax.psum(jnp.broadcast_to(valid_here, (COUNT_ROWS, D)), "dp")
    valid_total = valid_all[0, 0]
    parts_out = w_output.shape[2] // w_value.shape[2]
    output_local = w_output.reshape(rows, parts_out, w_value.shape[2], -1)
    output_local = [output_local[:, part].reshape(-1, w_output.shape[-1]) for part in range(parts_out)]
    near = rows == 2 and rows == blocks_here and cols == 4
    n_value, n_shared, n_reset, n_hidden = (
        weight.shape[-1] for weight in (w_value, w_shared, w_reset, w_hidden)
    )
    n_out = w_output.shape[-1]
    skip_value = n_value + n_shared
    front_weights = gather_weights(
        jnp.concatenate(
            [local_matrix([w_value, w_shared])]
            + output_local
            + [local_matrix([w_reset, w_hidden, w_update])],
            axis=1,
        )
    )
    shared_weights = front_weights[:, :, n_value:skip_value]
    rest_weights = front_weights[:, :, skip_value:]
    inner_local, down_local = local_matrix([w_gate, w_up]), local_matrix([w_down])
    deep_down = w_down.shape[2]
    if near:
        sides = [[[], []], [[], []], [[], []]]
        for start, count, side, lane, width, column in packed_pieces(rows, deep_down, n_out):
            piece = down_local[start : start + count, column : column + width]
            sides[lane // n_out][side // UNIT].append(piece)
        columns = [jnp.concatenate(tops + bottoms, axis=0) for tops, bottoms in sides]
        inner_weights = [gather_weights(jnp.concatenate([inner_local] + columns, axis=1))]
    else:
        inner_weights = [gather_weights(inner_local), gather_weights(down_local)]
    feat_share, z_share = final_gain.shape[0], query_gain.shape[0]

    def whole_vector(start, share):
        return vectors[:, start : start + share].reshape(-1)

    gain_all = whole_vector(0, feat_share)
    bias_all = whole_vector(feat_share, feat_share)
    query_gain_all = whole_vector(2 * feat_share, z_share)
    query_bias_all = whole_vector(2 * feat_share + z_share, z_share)
    key_gain_all = whole_vector(2 * feat_share + 2 * z_share, z_share)

    half, pieces = query_pieces(group, tokens, member)
    positions = jnp.concatenate([chunk * half + jnp.arange(half) for chunk, offset in pieces])
    valid_mask = (positions < block_len[my_block]).astype(jnp.float32)

    send_normed, send_mixed, send_plain, *saved = front_forward(
        layer_input, teacher, state_params, channel_params, bounds, places, devices
    )
    feats = layer_input.shape[0]
    if near:
        block_normed, mixed_low = spread_sources(send_normed, send_mixed, group)
    else:
        whole_normed = exchange(send_normed).reshape(devices * feats, tokens)
        block_normed = lax.dynamic_slice_in_dim(
            lax.all_gather(swap_blocks(whole_normed, rows, cols), grid, axis=0),
            my_block * group,
            group,
            0,
        )
        mixed_low = swap_blocks(
            exchange(send_mixed).reshape(devices * feats, tokens), rows, cols
        )
    skip_out = parts_out * n_out
    shared = project(shared_weights, mixed_low)
    mixed_out = [
        contract_first(rest_weights[part, :, skip_out:], mixed_low) for part in range(rows)
    ]

    def mixed_slice(start, count):
        return jnp.concatenate([piece[start : start + count] for piece in mixed_out], axis=0)

    reset_pre = mixed_slice(0, n_reset)
    hidden_pre = mixed_slice(n_reset, n_hidden)
    update_pre = mixed_slice(n_reset + n_hidden, n_hidden)
    queries = (shared * query_gain_all[:, None] + query_bias_all[:, None]).astype(bf16)
    keys_low = (shared * key_gain_all[:, None]).astype(bf16)
    if near:
        block_keys = gather_members(keys_low)
    else:
        block_keys = lax.dynamic_slice_in_dim(
            lax.all_gather(keys_low, grid, axis=0), my_block * group, group, 0
        )
    values_low, value_bends = block_values(front_weights, block_normed, n_value)
    send_plain, block_keys = barrier((send_plain, block_keys))
    plain = exchange(send_plain)
    input_slots = plain[:, 0].reshape(devices * feats, tokens).astype(jnp.float32)
    teacher_slots = plain[:, 1].reshape(devices * feats, tokens)

    attended, logs = attention_forward(
        member[None], queries, block_keys, values_low, group
    )
    reset_act = silu(reset_pre)
    att_in = (attended * reset_act).astype(bf16)
    att_in = att_in.reshape(rows, cols, parts_out, -1, tokens).transpose(2, 1, 0, 3, 4)
    att_in = att_in.reshape(parts_out, -1, tokens)
    summed = hidden_pre
    for part in range(parts_out):
        summed = summed + project(
            rest_weights[:, :, part * n_out : (part + 1) * n_out], att_in[part]
        )
    hidden_act = silu(summed)
    gate_act = jax.nn.sigmoid(update_pre)
    first_out = input_slots + gate_act * (hidden_act - input_slots)
    factor = slot_count * dps / valid_total
    (
        output_low,
        loss_rows,
        final_norm,
        inner_act,
        out_low,
        inner_grads,
        first_grad,
        final_gain_part,
        final_bias_part,
    ) = inner_layer(
        rows,
        cols,
        first_out,
        teacher_slots,
        valid_mask[None],
        factor[None],
        gain_all[:, None],
        bias_all[:, None],
        inner_weights,
        w_gate.shape[-1] + w_up.shape[-1],
        rows * w_gate.shape[-1],
    )
    loss_part = jnp.sum(loss_rows)

    def scatter_products(products):
        shaped = products.reshape((devices,) + products.shape[2:])
        return lax.psum_scatter(shaped, grid, scatter_dimension=0, tiled=True)[0]

    def scatter_weight(product_list, rank):
        shaped = product_list.reshape(devices, rows * rank, product_list.shape[-1])
        return lax.psum_scatter(shaped, grid, scatter_dimension=0, tiled=True)[0]

    if near:
        inner_products = packed_products(
            rows, cols, final_norm, inner_grads, inner_act, out_low
        )
        inner_products, first_grad = barrier((inner_products, first_grad))
        inner_sums = (scatter_products(inner_products),)
    else:
        inner_sums = (
            scatter_products(local_products(rows, cols, final_norm, inner_grads)),
            scatter_products(local_products(rows, cols, inner_act, out_low)),
        )
    direct = exchange(
        jnp.stack(
            [
                (first_grad * (1.0 - gate_act)).astype(bf16).reshape(devices, feats, tokens),
                output_low.reshape(devices, feats, tokens),
            ],
            axis=1,
        )
    )
    update_grad = (first_grad * (hidden_act - input_slots) * gate_act * (1.0 - gate_act)).astype(
        bf16
    )
    summed_grad = (first_grad * gate_act * silu_slope(summed)).astype(bf16)
    att_grad = jnp.stack(
        [
            project_back(rest_weights[:, :, part * n_out : (part + 1) * n_out], summed_grad)
            for part in range(parts_out)
        ]
    )
    att_grad = att_grad.reshape(parts_out, cols, rows, feats, tokens).transpose(2, 1, 0, 3, 4)
    att_grad = att_grad.reshape(-1, tokens)
    attended_grad = (att_grad * reset_act).astype(bf16)
    reset_grad = (att_grad * attended * silu_slope(reset_pre)).astype(bf16)
    mixed_grads = jnp.concatenate(
        [piece.reshape(rows, -1, tokens) for piece in (reset_grad, summed_grad, update_grad)],
        axis=1,
    )
    rest_products = [
        jnp.concatenate(columns, axis=1)
        for columns in zip(
            *[weight_products(att_in[part], summed_grad, rows) for part in range(parts_out)],
            weight_products(mixed_low, mixed_grads, rows),
        )
    ]
    rest_products, attended_grad = barrier((jnp.stack(rest_products), attended_grad))
    rest_sum = scatter_weight(rest_products, w_value.shape[2])
    query_grad, key_parts, value_parts = attention_backward(
        member[None], queries, block_keys, values_low, value_bends, attended_grad, logs, group
    )
    key_parts, direct = barrier((key_parts, direct))
    if near:
        key_grad = reduce_members(key_parts)
    else:
        spread = lax.dynamic_update_slice_in_dim(
            jnp.zeros((devices,) + key_parts.shape[1:], bf16), key_parts, my_block * group, 0
        )
        key_grad = lax.psum_scatter(spread, grid, scatter_dimension=0, tiled=True)[0]
        key_grad = key_grad.astype(jnp.float32)
    normed_back = block_values_back(front_weights, value_parts, n_value)
    shared_grad = (
        query_grad * query_gain_all[:, None] + key_grad * key_gain_all[:, None]
    ).astype(bf16)
    query_gain_part = jnp.sum(query_grad * shared, axis=1)
    query_bias_part = jnp.sum(query_grad, axis=1)
    key_gain_part = jnp.sum(key_grad * shared, axis=1)
    mixed_back = project_back(
        rest_weights[:, :, skip_out:], mixed_grads.reshape(-1, tokens)
    ) + project_back(shared_weights, shared_grad)
    mixed_back = mixed_back.astype(bf16)
    if near:
        normed_grads, mixed_backs = collect_grads(normed_back, mixed_back, devices)
    else:
        spread = lax.dynamic_update_slice_in_dim(
            jnp.zeros((devices,) + normed_back.shape[1:], bf16), normed_back, my_block * group, 0
        )
        spread = spread.reshape(devices, cols, rows, feats, tokens).transpose(2, 1, 0, 3, 4)
        normed_grads = lax.psum_scatter(
            spread.reshape((devices, devices, feats, tokens)), grid, scatter_dimension=0, tiled=True
        )[0]
        mixed_backs = exchange(
            swap_blocks(mixed_back, cols, rows).reshape(devices, feats, tokens)
        )
    inner_sums, valid_all, normed_grads = barrier((inner_sums, valid_all, normed_grads))
    inner_sums = lax.psum(inner_sums, "dp")
    groups = feats // GS
    shares = [(0, groups)]
    if groups % 2 == 0:
        shares = [(0, groups // 2), (groups // 2, groups // 2)]
    filled = ()
    for first, count in shares:
        if filled:
            rest_sum, inner_sums, filled = barrier((rest_sum, inner_sums, filled))
            rest_sum = lax.psum(rest_sum, "dp")
        filled = front_backward(
            layer_input,
            state_params,
            channel_params,
            bounds,
            places,
            devices,
            normed_grads,
            mixed_backs,
            direct,
            saved,
            first,
            count,
            filled,
        )
    layer_output, input_grad, state_grads, channel_grads = filled
    param_grads = front_parameter_grads(state_grads, channel_grads, ema_rate, ema_input)

    value_part = block_values_products(rows, block_normed, value_parts)
    shared_part = weight_products(mixed_low, shared_grad, rows)
    value_products = jnp.concatenate([value_part, jnp.stack(shared_part)], axis=2)
    value_sum = scatter_weight(value_products, w_value.shape[2])
    if len(shares) == 1:
        rest_sum, inner_sums = barrier((rest_sum, inner_sums))
        rest_sum = lax.psum(rest_sum, "dp")
    value_sum, rest_sum = barrier((value_sum, rest_sum))
    value_sum = lax.psum(value_sum, "dp")

    vector_parts = [final_gain_part, final_bias_part, query_gain_part, query_bias_part, key_gain_part]
    vector_parts = jnp.concatenate(
        [part.reshape(devices, -1) for part in vector_parts]
        + [jnp.broadcast_to(loss_part, (devices, 1))],
        axis=1,
    )
    vector_sums = jnp.sum(exchange(vector_parts), axis=0)
    *param_sums, small = lax.psum((*param_grads, vector_sums), "dp")
    loss_value = small[-1] / (2.0 * valid_total * D)

    def split_columns(array_in, weight_list):
        results = []
        offset = 0
        for weight in weight_list:
            count = weight.shape[-1]
            piece = array_in[:, offset : offset + count].astype(jnp.float32)
            results.append(piece.reshape(weight.shape))
            offset += count
        return results

    value_g, shared_g = split_columns(value_sum, [w_value, w_shared])
    reset_g, hidden_g, update_g = split_columns(
        rest_sum[:, skip_out:], [w_reset, w_hidden, w_update]
    )
    output_g = jnp.stack(
        [
            rest_sum[:, part * n_out : (part + 1) * n_out].reshape(rows, -1, n_out)
            for part in range(parts_out)
        ],
        axis=1,
    )
    output_g = output_g.astype(jnp.float32).reshape(w_output.shape)
    gate_g, up_g = split_columns(inner_sums[0], [w_gate, w_up])
    if near:
        packed_down = inner_sums[0][:, w_gate.shape[-1] + w_up.shape[-1] :]
        strips = {}
        for start, count, side, lane, width, column in packed_pieces(rows, deep_down, n_out):
            strips.setdefault(start, []).append(
                packed_down[side : side + count, lane : lane + width]
            )
        down_g = jnp.concatenate(
            [jnp.concatenate(strips[start], axis=1) for start in sorted(strips)], axis=0
        )
    else:
        down_g = inner_sums[1]
    down_g = down_g.astype(jnp.float32).reshape(w_down.shape)
    return (
        layer_output,
        loss_value,
        input_grad,
        *param_sums,
        value_g,
        shared_g,
        reset_g,
        hidden_g,
        update_g,
        small[2 * feat_share : 2 * feat_share + z_share],
        small[2 * feat_share + z_share : 2 * feat_share + 2 * z_share],
        small[2 * feat_share + 2 * z_share : 2 * feat_share + 3 * z_share],
        output_g,
        small[:feat_share],
        small[feat_share : 2 * feat_share],
        gate_g,
        up_g,
        down_g,
    )


def solution(mesh):
    in_specs = (
        P(("row", "col"), "dp"),
        P(("row", "col"), "dp"),
        P("dp"),
        P("dp"),
        P(("row", "col")),
        P(("row", "col")),
        P(("row", "col"), None),
        P(("row", "col"), None),
        P(("row", "col"), None),
        P(("row", "col"), None),
        P(("row", "col"), None),
        P(("row", "col")),
        P(None, "col", None, "row"),
        P(None, "col", None, "row"),
        P(None, "col", None, "row"),
        P(None, "col", None, "row"),
        P(None, "col", None, "row"),
        P(("row", "col")),
        P(("row", "col")),
        P(("row", "col")),
        P(None, "col", None, "row"),
        P(("row", "col")),
        P(("row", "col")),
        P(None, "col", None, "row"),
        P(None, "col", None, "row"),
        P(None, "col", None, "row"),
    )
    out_specs = (
        P(("row", "col"), "dp"),
        P(),
        P(("row", "col"), "dp"),
        P(("row", "col")),
        P(("row", "col")),
        P(("row", "col"), None),
        P(("row", "col"), None),
        P(("row", "col"), None),
        P(("row", "col"), None),
        P(("row", "col"), None),
        P(("row", "col")),
        P(None, "col", None, "row"),
        P(None, "col", None, "row"),
        P(None, "col", None, "row"),
        P(None, "col", None, "row"),
        P(None, "col", None, "row"),
        P(("row", "col")),
        P(("row", "col")),
        P(("row", "col")),
        P(None, "col", None, "row"),
        P(("row", "col")),
        P(("row", "col")),
        P(None, "col", None, "row"),
        P(None, "col", None, "row"),
        P(None, "col", None, "row"),
    )
    return jax.shard_map(shards, mesh=mesh, in_specs=in_specs, out_specs=out_specs, check_vma=False)
```
